256 devices in a mesh: tm: 32 (over y, x, core), sr: 8 (over z).
Axes of the slice: x: 4, y: 4, z: 8, core: 2. Of those that a mesh axis runs over, the one named last changes fastest.
Arguments:
- observations: bfloat16 [4096, 65536], P(None, ('sr', 'tm')), may hold values from -6 to 6
- loadings: float32 [65536, 128], P(('sr', 'tm')), may hold values from -0.00036621094 to 0.00036621094
- noise_precision: float32 [65536], P(('sr', 'tm')), may hold values from 0.5 to 4
- transition: float32 [128, 128], replicated, may hold values from -1 to 1, as said below
- filter_cov: float32 [128, 128], replicated, may hold values from -1 to 1, as said below
- smoother_gain: float32 [128, 128], replicated, may hold values from -1 to 1, as said below
- smoothed_cov: float32 [128, 128], replicated, may hold values from -1 to 1, as said below
Outputs:
- smoothed_factors: float32 [4096, 128], P('tm')
- new_loadings: float32 [65536, 128], P(('sr', 'tm'))
- new_transition: float32 [128, 128], replicated
The draws below stay inside these ranges and needn't reach their ends.
Inputs may be any that keep to these rules, and one draw needn't show every extreme that they name: `transition`: the spectral radius is below one. `filter_cov`: symmetric positive definite. `smoother_gain`: the spectral radius is below one. `smoothed_cov`: symmetric positive definite.
All inputs are finite; a program needn't handle non-finite values.
Results may differ from the reference program's by a relative error of at most 0.00175.
The reference program's roundings to bfloat16 on the way (of `scaled` and `factors_b`) count: a program that leaves them out, or rounds other values in their place, can miss the bound.
Values may be sent and summed in bfloat16 or wider, within the bound.
No kernel may reach another device: no remote copies, remote signals or barrier semaphores. Data moves between devices by JAX's collectives and lax.ppermute only.
A program may use at most 64 MiB of HBM per device.

```python
import math
import jax
import jax.numpy as jnp
from jax import lax

SERIES = 65536
FACTORS = 128
TIME = 4096


def modal_parts(key):
    base = jax.random.fold_in(key, 4711)
    subkeys = jax.random.split(base, 10)
    normal_basis = jax.random.normal(subkeys[0], (FACTORS, FACTORS), jnp.float32)
    basis, unused = jnp.linalg.qr(normal_basis)
    slowness = jax.random.randint(subkeys[1], (FACTORS // 2,), 0, 2) > 0
    return (basis, slowness, subkeys)


def rotation_blocks(radius, angle):
    evens = jnp.arange(0, FACTORS, 2)
    cosine = radius * jnp.cos(angle)
    sine = radius * jnp.sin(angle)
    matrix = jnp.zeros((FACTORS, FACTORS), jnp.float32)
    matrix = matrix.at[evens, evens].set(cosine).at[evens, evens + 1].set(-sine)
    matrix = matrix.at[evens + 1, evens].set(sine).at[evens + 1, evens + 1].set(cosine)
    return matrix


def turning(basis, slowness, first_key, second_key, angle_key):
    half = FACTORS // 2
    slow_radius = jnp.exp(-jax.random.uniform(first_key, (half,), jnp.float32, 0.1, 0.6) / TIME)
    fast_radius = jnp.exp(-1.0 / jax.random.uniform(second_key, (half,), jnp.float32, 30.0, 50.0))
    radius = jnp.where(slowness, slow_radius, fast_radius)
    angle = jax.random.uniform(angle_key, (half,), jnp.float32, 0.3, 2.8)
    inner = rotation_blocks(radius, angle)
    return jnp.dot(jnp.dot(basis, inner, precision=lax.Precision.HIGHEST), basis.T, precision=lax.Precision.HIGHEST)


def draw_transition(key, part):
    basis, slowness, subkeys = modal_parts(key)
    return turning(basis, slowness, subkeys[2], subkeys[3], subkeys[4])


def draw_smoother_gain(key, part):
    basis, slowness, subkeys = modal_parts(key)
    return turning(basis, slowness, subkeys[5], subkeys[6], subkeys[7])


def draw_filter_cov(key, part):
    basis, slowness, subkeys = modal_parts(key)
    values = jnp.exp(jax.random.uniform(subkeys[8], (FACTORS,), jnp.float32, jnp.log(0.2), 0.0))
    return jnp.dot(basis * values[None, :], basis.T, precision=lax.Precision.HIGHEST)


def draw_smoothed_cov(key, part):
    basis, slowness, subkeys = modal_parts(key)
    values = jax.random.uniform(subkeys[9], (FACTORS,), jnp.float32, 0.3, 1.0)
    return jnp.dot(basis * values[None, :], basis.T, precision=lax.Precision.HIGHEST)


def block_levels(own_key, extent, shards, low, top_value):
    loudness = 1.0
    for axis_at, shards_of in shards:
        draws = jax.random.uniform(jax.random.fold_in(jax.random.fold_in(own_key, 6), axis_at), (shards_of,), jnp.float32, low / len(shards), top_value / len(shards))
        loudness = loudness * jnp.repeat(jnp.exp(draws), extent[axis_at] // shards_of).reshape((-1,) + (1,) * (len(extent) - 1 - axis_at))
    return loudness


def normal_values(key, dims, width, bound, cuts=(), dtype=jnp.bfloat16):
    level = block_levels(key, dims, cuts, -0.22, 0.18) if cuts else 1.0
    values = jax.random.normal(key, dims, jnp.float32) * width * level
    return jnp.minimum(jnp.maximum(values, -bound), bound).astype(dtype)


def setup_inputs(seed: int = 0) -> dict:
    splits = jax.random.split(jax.random.key(seed), 8)
    observations = normal_values(splits[0], (TIME, SERIES), 1.0, 6.0, ((1, 256),))
    loadings = normal_values(splits[1], (SERIES, FACTORS), (SERIES * TIME) ** -0.5, 0.00036621094, ((0, 256),), jnp.float32)
    noise_precision = jnp.clip(jnp.exp(math.log(4.0) - 2.0794415 * jax.random.uniform(splits[2], (SERIES,), jnp.float32) ** block_levels(splits[2], (SERIES,), ((0, 256),), -0.2, 0.2)), 0.5, 4.0)
    transition = draw_transition(jax.random.fold_in(splits[7], 71), 0)
    filter_cov = draw_filter_cov(jax.random.fold_in(splits[7], 71), 0)
    smoother_gain = draw_smoother_gain(jax.random.fold_in(splits[7], 71), 0)
    smoothed_cov = draw_smoothed_cov(jax.random.fold_in(splits[7], 71), 0)
    return dict(observations=observations, loadings=loadings, noise_precision=noise_precision, transition=transition, filter_cov=filter_cov, smoother_gain=smoother_gain, smoothed_cov=smoothed_cov)


precise = lax.Precision.HIGHEST

def dot_high(left, right):
    return jnp.dot(left.astype(jnp.float32), right.astype(jnp.float32), precision=precise, preferred_element_type=jnp.float32)

def reference(observations, loadings, noise_precision, transition, filter_cov, smoother_gain, smoothed_cov):
    scaled = (noise_precision[:, None] * loadings).astype(jnp.bfloat16)
    proj = jnp.dot(observations.astype(jnp.float32), scaled.astype(jnp.float32), preferred_element_type=jnp.float32)
    info = dot_high(loadings.T, noise_precision[:, None] * loadings)
    closed = transition - dot_high(filter_cov, dot_high(info, transition))
    inputs = dot_high(proj, filter_cov.T)

    def forward(state, drive):
        following = dot_high(closed, state) + drive
        return (following, following)
    unused, filtered = lax.scan(forward, jnp.zeros((FACTORS,), jnp.float32), inputs)
    coupled = dot_high(smoother_gain, transition)
    back = filtered - dot_high(filtered, coupled.T)
    back = back.at[TIME - 1].set(filtered[TIME - 1])

    def backward(state, drive):
        following = dot_high(smoother_gain, state) + drive
        return (following, following)
    unused, smoothed = lax.scan(backward, jnp.zeros((FACTORS,), jnp.float32), back, reverse=True)
    factors_b = smoothed.astype(jnp.bfloat16)
    cross = jnp.einsum('ts,tk->sk', observations.astype(jnp.float32), factors_b.astype(jnp.float32), preferred_element_type=jnp.float32)
    total = dot_high(smoothed.T, smoothed) + TIME * smoothed_cov
    previous = dot_high(smoothed[:-1].T, smoothed[:-1]) + (TIME - 1) * smoothed_cov
    lagged = dot_high(smoothed[1:].T, smoothed[:-1]) + (TIME - 1) * dot_high(smoothed_cov, smoother_gain.T)
    total_factor = jnp.linalg.cholesky(total)
    new_loadings = jax.scipy.linalg.cho_solve((total_factor, True), cross.T).T
    previous_factor = jnp.linalg.cholesky(previous)
    new_transition = jax.scipy.linalg.cho_solve((previous_factor, True), lagged.T).T
    return (smoothed, new_loadings, new_transition)
```

```python
import functools

import jax
import jax.numpy as jnp
from jax import lax
from jax.experimental import pallas as pl
from jax.experimental.pallas import tpu as pltpu
from jax.sharding import Mesh
from jax.sharding import PartitionSpec as P

Y, X, CORE, Z = "tm_0", "tm_1", "tm_2", "sr"
TM = (Y, X, CORE)
SR_TM = (Z, Y, X, CORE)

STEPS = 16
f32 = jnp.float32
bf16 = jnp.bfloat16
precise = lax.Precision.HIGHEST


def thirds(v):
    a = v.astype(bf16)
    rest = v - a.astype(f32)
    b = rest.astype(bf16)
    c = (rest - b.astype(f32)).astype(bf16)
    return a, b, c


def right(w):
    a, b, c = thirds(w)
    both = jnp.concatenate([a, b], axis=1)
    if w.shape[0] <= 128:
        return both, (jnp.concatenate([c, a], axis=0),)
    return both, (c, a)


def plain(a, b):
    return jnp.dot(a, b, preferred_element_type=f32)


def times(v, w):
    both, small = w
    n = both.shape[1] // 2
    a, b, c = thirds(v)
    p, q = plain(a, both), plain(b, both)
    if len(small) == 1:
        least = plain(jnp.concatenate([a, c], axis=1), small[0])
    else:
        least = plain(a, small[0]) + plain(c, small[1])
    return p[:, :n] + (p[:, n:] + q[:, :n] + (q[:, n:] + least))


def high(a, b):
    return times(a, right(b))


def contracted(a, b):
    return lax.dot_general(a, b, (((0,), (0,)), ((), ())), preferred_element_type=f32)


def moved(v, shift, row):
    n = v.shape[0]
    keep = (row >= shift) if shift > 0 else (row < n + shift)
    return jnp.where(keep, pltpu.roll(v, shift % n, 0), 0.0)


def powers(a, n):
    found = [a]
    while len(found) < STEPS:
        more = high(jnp.concatenate(found, axis=0), found[-1])
        found = found + [more[i * n : (i + 1) * n] for i in range(len(found))]
    return found


def scan_kernel(
    core_ref, own_ref, other_ref, ft_ref, kt_ref, jt_ref, cov_ref,
    x_ref, total_ref, previous_ref, lagged_ref, loc_ref, mat_ref,
):
    n = ft_ref.shape[0]
    groups = own_ref.shape[0]
    rows = x_ref.shape[0] // (2 * groups)
    blocks = x_ref.shape[0] // STEPS
    length = x_ref.shape[0]
    first = core_ref[0] == 0
    ft, kt, jt, cov = ft_ref[...], kt_ref[...], jt_ref[...], cov_ref[...]
    info = jnp.concatenate([own_ref[g, rows:] for g in range(groups)], axis=0)
    eye = (
        lax.broadcasted_iota(jnp.int32, (n, n), 0) == lax.broadcasted_iota(jnp.int32, (n, n), 1)
    ).astype(f32)
    row = lax.broadcasted_iota(jnp.int32, (blocks, n), 0)
    a = ft - high(high(ft, info), kt)
    b = eye - high(ft, jt)
    apow = powers(a, n)
    jpow = powers(jt, n)

    def drive(j):
        def half(ref):
            parts = [ref[g, pl.ds(j, rows // STEPS, stride=STEPS), :] for g in range(groups)]
            return jnp.concatenate(parts, axis=0)

        own, other = half(own_ref), half(other_ref)
        return jnp.concatenate(
            [jnp.where(first, own, other), jnp.where(first, other, own)], axis=0
        )

    step = right(jnp.concatenate([a, kt], axis=0))
    state = times(drive(0), right(kt))
    loc_ref[0] = state
    for j in range(1, STEPS):
        state = times(jnp.concatenate([state, drive(j)], axis=1), step)
        loc_ref[j] = state
    enter = state
    back = right(jnp.concatenate([jt, b], axis=0))
    both = lambda j: jnp.concatenate([loc_ref[j], apow[j]], axis=0)
    out = times(both(STEPS - 1), right(b))
    for j in range(STEPS - 1, -1, -1):
        if j < STEPS - 1:
            out = times(jnp.concatenate([out, both(j)], axis=1), back)
        loc_ref[j] = out[:blocks]
        mat_ref[j] = out[blocks:]
    power, shift = apow[STEPS - 1], 1
    while shift < blocks:
        w = right(power)
        enter = enter + times(moved(enter, shift, row), w)
        shift *= 2
        if shift < blocks:
            power = times(power, w)
    e = moved(enter, 1, row)
    after = high(jnp.where(row == blocks - 1, enter, 0.0), ft)
    z = loc_ref[0] + high(e, mat_ref[0]) + high(after, jpow[STEPS - 1])
    power, shift = jpow[STEPS - 1], 1
    while shift < blocks:
        w = right(power)
        z = z + times(moved(z, -shift, row), w)
        shift *= 2
        if shift < blocks:
            power = times(power, w)
    mix = jnp.concatenate([e, moved(z, -1, row) + after], axis=1)
    for j in range(STEPS):
        x = z
        if j > 0:
            x = loc_ref[j] + high(mix, jnp.concatenate([mat_ref[j], jpow[STEPS - 1 - j]], axis=0))
        loc_ref[j] = x
        x_ref[pl.ds(j, blocks, stride=STEPS), :] = x
    sums = jnp.zeros((n, 2 * n), f32)
    for j in range(STEPS):
        x = loc_ref[j]
        prior = moved(loc_ref[STEPS - 1], 1, row) if j == 0 else loc_ref[j - 1]
        xa, xb, _ = thirds(x)
        pa, pb, _ = thirds(prior)
        pair = jnp.concatenate([xa, pa], axis=1)
        rest = jnp.concatenate([xb, pb], axis=1)
        sums = sums + contracted(xa, pair) + (contracted(xb, pair) + contracted(xa, rest))
    last = jnp.where(row == blocks - 1, loc_ref[STEPS - 1], 0.0)
    la, lb, _ = thirds(last)
    ends = contracted(la, la) + (contracted(lb, la) + contracted(la, lb))
    total_ref[...] = sums[:, :n] + length * cov
    previous_ref[...] = (sums[:, :n] - ends) + (length - 1) * cov
    lagged_ref[...] = sums[:, n:] + (length - 1) * high(cov, jt)


def scanned(core, own, other, ft, kt, jt, cov, length):
    n = ft.shape[0]
    square = jax.ShapeDtypeStruct((n, n), f32)
    vmem = pl.BlockSpec(memory_space=pltpu.VMEM)
    return pl.pallas_call(
        scan_kernel,
        out_shape=(jax.ShapeDtypeStruct((length, n), f32), square, square, square),
        in_specs=[pl.BlockSpec(memory_space=pltpu.SMEM)] + [vmem] * 6,
        out_specs=[vmem] * 4,
        scratch_shapes=[
            pltpu.VMEM((STEPS, length // STEPS, n), f32),
            pltpu.VMEM((STEPS, n, n), f32),
        ],
        compiler_params=pltpu.CompilerParams(vmem_limit_bytes=44 * 1024 * 1024),
        cost_estimate=pl.CostEstimate(flops=10**10, bytes_accessed=5 * 10**6, transcendentals=0),
        name="scan",
    )(core, own, other, ft, kt, jt, cov)


def swept(mats, n):
    row8 = lax.broadcasted_iota(jnp.int32, (8, n), 0)
    lane = lax.broadcasted_iota(jnp.int32, (1, n), 1)
    mats = [[m[8 * g : 8 * g + 8] for g in range(n // 8)] for m in mats]
    for k in range(n):
        found = []
        for m in mats:
            g, o = divmod(k, 8)
            pivot_row = m[g][o : o + 1, :]
            d = 1.0 / pivot_row[:, k : k + 1]
            s = jnp.where(lane == k, d, pivot_row * d)
            new = []
            for i, t in enumerate(m):
                u = jnp.where(lane == k, 0.0, t) - t[:, k : k + 1] * s
                new.append(jnp.where(row8 == o, s, u) if i == g else u)
            found.append(new)
        mats = found
    return [jnp.concatenate(m, axis=0) for m in mats]


def inverse_kernel(total_ref, previous_ref, lagged_ref, inverse_ref, transition_ref):
    inverse, other = swept([total_ref[...], previous_ref[...]], total_ref.shape[0])
    inverse_ref[...] = inverse
    transition_ref[...] = high(lagged_ref[...], other)


def inverted(total, previous, lagged):
    vmem = pl.BlockSpec(memory_space=pltpu.VMEM)
    square = jax.ShapeDtypeStruct(total.shape, f32)
    return pl.pallas_call(
        inverse_kernel,
        out_shape=(square, square),
        in_specs=[vmem] * 3,
        out_specs=[vmem] * 2,
        compiler_params=pltpu.CompilerParams(vmem_limit_bytes=16 * 1024 * 1024),
        cost_estimate=pl.CostEstimate(flops=10**9, bytes_accessed=3 * 10**5, transcendentals=0),
        name="inverse",
    )(total, previous, lagged)


def turned(value, axis, steps):
    count = lax.axis_size(axis)
    return lax.ppermute(value, axis, [(i, (i + steps) % count) for i in range(count)])


def over_z(value):
    count = lax.axis_size(Z)
    value = value + lax.ppermute(value, Z, [(i, i ^ 1) for i in range(count)])
    arrived = [turned(value, Z, 2 * k) for k in range(1, count // 2)]
    return sum(arrived, value)


def local(
    observations, loadings, noise_precision, transition, filter_cov, smoother_gain, smoothed_cov
):
    core = lax.axis_index(CORE)
    position = lax.axis_index(TM)
    length = observations.shape[0]
    width = transition.shape[0]
    half = length // 2
    groups = lax.axis_size((Y, X))
    rows = half // groups
    extra = width // groups
    weighted = noise_precision[:, None] * loadings
    scaled = weighted.astype(bf16)

    def projected(which):
        window = lax.dynamic_slice_in_dim(observations, which * half, half, 0)
        return jnp.dot(window, scaled, preferred_element_type=f32)

    info_part = jnp.dot(loadings.T, weighted, precision=precise, preferred_element_type=f32)
    info_part = info_part + turned(info_part, CORE, 1)
    mine = projected(core) + turned(projected(1 - core), CORE, 1)
    pieces = jnp.concatenate(
        [mine.reshape(groups, rows, width), info_part.reshape(groups, extra, width)], axis=1
    )
    arrived = lax.all_to_all(pieces, (Y, X), split_axis=0, concat_axis=0, tiled=True)
    block = over_z(arrived.sum(axis=0))
    copies = jnp.broadcast_to(block, (groups, *block.shape))
    own = lax.all_to_all(copies, (Y, X), split_axis=0, concat_axis=0, tiled=True)
    other = turned(own, CORE, 1)
    smoothed, total, previous, lagged = scanned(
        core[None].astype(jnp.int32), own, other,
        transition.T, filter_cov.T, smoother_gain.T, smoothed_cov, length,
    )
    inverse, new_transition = inverted(total, previous, lagged)
    cross = jnp.einsum(
        "ts,tk->sk", observations, smoothed.astype(bf16), preferred_element_type=f32
    )
    new_loadings = jnp.dot(cross, inverse, precision=precise, preferred_element_type=f32)
    steps_dev = length // lax.axis_size(TM)
    shown = lax.dynamic_slice_in_dim(smoothed, position * steps_dev, steps_dev, 0)
    return (shown, new_loadings, new_transition)


def solution(mesh):
    split = Mesh(mesh.devices.reshape(4, 4, 2, mesh.shape["sr"]), (Y, X, CORE, Z))
    in_specs = (P(None, SR_TM), P(SR_TM, None), P(SR_TM), P(), P(), P(), P())
    out_specs = (P(TM, None), P(SR_TM, None), P())
    return jax.shard_map(local, mesh=split, in_specs=in_specs, out_specs=out_specs, check_vma=False)
```

```python
import jax
import jax.numpy as jnp
from jax import lax
from jax.experimental import pallas as pl
from jax.experimental.pallas import tpu as pltpu
from jax.sharding import Mesh
from jax.sharding import PartitionSpec as P

Y, X, CORE, Z = "tm_0", "tm_1", "tm_2", "sr"
TM = (Y, X, CORE)
SR_TM = (Z, Y, X, CORE)

STEPS = 8
SQUARINGS = 7
f32 = jnp.float32
bf16 = jnp.bfloat16
precise = lax.Precision.HIGHEST


def thirds(v):
    a = v.astype(bf16)
    rest = v - a.astype(f32)
    b = rest.astype(bf16)
    c = (rest - b.astype(f32)).astype(bf16)
    return a, b, c


def right(w):
    a, b, c = thirds(w)
    both = jnp.concatenate([a, b], axis=1)
    if w.shape[0] <= 128:
        return both, (jnp.concatenate([c, a], axis=0),)
    return both, (c, a)


def plain(a, b):
    return jnp.dot(a, b, preferred_element_type=f32)


def times(v, w):
    return times_split(thirds(v), w)


def times_split(v, w):
    both, small = w
    n = both.shape[1] // 2
    a, b, c = v
    p, q = plain(a, both), plain(b, both)
    if len(small) == 1:
        least = plain(jnp.concatenate([a, c], axis=1), small[0])
    else:
        least = plain(a, small[0]) + plain(c, small[1])
    return p[:, :n] + (p[:, n:] + q[:, :n] + (q[:, n:] + least))


def high(a, b):
    return times(a, right(b))


def contracted(a, b):
    return lax.dot_general(a, b, (((0,), (0,)), ((), ())), preferred_element_type=f32)


def moved(v, shift, row):
    n = v.shape[0]
    keep = (row >= shift) if shift > 0 else (row < n + shift)
    return jnp.where(keep, pltpu.roll(v, shift % n, 0), 0.0)


def powers(a, n):
    found = [a]
    while len(found) < STEPS:
        more = high(jnp.concatenate(found, axis=0), found[-1])
        found = found + [more[i * n : (i + 1) * n] for i in range(len(found))]
    return found


def kept(blocks_at, count=1):
    both = blocks_at[0]
    small = blocks_at[1]
    if count == 1:
        return both, (jnp.concatenate([small, both[:, : both.shape[1] // 2]], axis=0),)
    return both, (small, both[:, : both.shape[1] // 2])


def beneath(*pieces):
    return tuple(jnp.concatenate(p, axis=0) for p in zip(*pieces))


def pieces_of(w):
    a, b, c = thirds(w)
    return jnp.concatenate([a, b], axis=1), c


def ready_kernel(ft_ref, kt_ref, jt_ref, cov_ref, both_ref, small_ref, drift_ref):
    n = ft_ref.shape[0]
    ft, kt, jt = ft_ref[...], kt_ref[...], jt_ref[...]
    eye = (
        lax.broadcasted_iota(jnp.int32, (n, n), 0) == lax.broadcasted_iota(jnp.int32, (n, n), 1)
    ).astype(f32)

    def put(at, w):
        both, small = pieces_of(w)
        both_ref[at] = both
        small_ref[at] = small

    put(0, kt)
    put(1, eye - high(ft, jt))
    raised = powers(jt, n)
    for k, w in enumerate(raised):
        put(2 + k, w)
    power = raised[-1]
    for k in range(STEPS + 2, both_ref.shape[0]):
        power = high(power, power)
        put(k, power)
    drift_ref[...] = high(cov_ref[...], jt)


def readied(ft, kt, jt, cov, length):
    n = ft.shape[0]
    count = 2 + STEPS + (length // STEPS).bit_length() - 2
    vmem = pl.BlockSpec(memory_space=pltpu.VMEM)
    return pl.pallas_call(
        ready_kernel,
        out_shape=(
            jax.ShapeDtypeStruct((count, n, 2 * n), bf16),
            jax.ShapeDtypeStruct((count, n, n), bf16),
            jax.ShapeDtypeStruct((n, n), f32),
        ),
        in_specs=[vmem] * 4,
        out_specs=[vmem] * 3,
        compiler_params=pltpu.CompilerParams(vmem_limit_bytes=16 * 1024 * 1024),
        cost_estimate=pl.CostEstimate(flops=10**9, bytes_accessed=2 * 10**6, transcendentals=0),
        name="ready",
    )(ft, kt, jt, cov)


def scan_kernel(
    core_ref, place_ref, own_ref, other_ref, both_ref, small_ref, ft_ref, kt_ref, cov_ref, drift_ref,
    x_ref, shown_ref, total_ref, previous_ref, lagged_ref, loc_ref, mat_ref,
):
    n = ft_ref.shape[0]
    groups = own_ref.shape[0]
    length = x_ref.shape[0]
    rows = length // (2 * groups)
    blocks = length // STEPS
    first = core_ref[0] == 0
    ft, cov = ft_ref[...], cov_ref[...]
    held = lambda k: (both_ref[k], small_ref[k])
    info = jnp.concatenate([own_ref[g, rows:] for g in range(groups)], axis=0)
    row = lax.broadcasted_iota(jnp.int32, (blocks, n), 0)
    a = ft - times(high(ft, info), kept(held(0)))
    apow = powers(a, n)

    def drive(j):
        def half(ref):
            parts = [ref[g, pl.ds(j, rows // STEPS, stride=STEPS), :] for g in range(groups)]
            return jnp.concatenate(parts, axis=0)

        own, other = half(own_ref), half(other_ref)
        return jnp.concatenate(
            [jnp.where(first, own, other), jnp.where(first, other, own)], axis=0
        )

    step = kept(beneath(pieces_of(a), held(0)), 2)
    state = times(drive(0), kept(held(0)))
    loc_ref[0] = state
    for j in range(1, STEPS):
        state = times(jnp.concatenate([state, drive(j)], axis=1), step)
        loc_ref[j] = state
    enter = state
    back = kept(beneath(held(2), held(1)), 2)
    both = lambda j: jnp.concatenate([loc_ref[j], apow[j]], axis=0)
    out = times(both(STEPS - 1), kept(held(1)))
    for j in range(STEPS - 1, -1, -1):
        if j < STEPS - 1:
            out = times(jnp.concatenate([out, both(j)], axis=1), back)
        loc_ref[j] = out[:blocks]
        mat_ref[j] = out[blocks:]
    power, shift = apow[STEPS - 1], 1
    while shift < blocks:
        w = right(power)
        enter = enter + times(moved(enter, shift, row), w)
        shift *= 2
        if shift < blocks:
            power = times(power, w)
    e = moved(enter, 1, row)
    after = high(jnp.where(row == blocks - 1, enter, 0.0), ft)
    z = loc_ref[0] + high(e, mat_ref[0]) + times(after, kept(held(1 + STEPS)))
    level, shift = 1 + STEPS, 1
    while shift < blocks:
        z = z + times(moved(z, -shift, row), kept(held(level)))
        shift *= 2
        level += 1
    mix = jnp.concatenate([e, moved(z, -1, row) + after], axis=1)
    mixed = thirds(mix)
    for j in range(STEPS):
        x = z
        if j > 0:
            w = kept(beneath(pieces_of(mat_ref[j]), held(1 + STEPS - j)), 2)
            x = loc_ref[j] + times_split(mixed, w)
        loc_ref[j] = x
        x_ref[pl.ds(j, blocks, stride=STEPS), :] = x
    sums = jnp.zeros((n, 2 * n), f32)
    for j in range(STEPS):
        x = loc_ref[j]
        prior = moved(loc_ref[STEPS - 1], 1, row) if j == 0 else loc_ref[j - 1]
        xa, xb, _ = thirds(x)
        pa, pb, _ = thirds(prior)
        pair = jnp.concatenate([xa, pa], axis=1)
        rest = jnp.concatenate([xb, pb], axis=1)
        sums = sums + contracted(xa, pair) + (contracted(xb, pair) + contracted(xa, rest))
    last = jnp.where(lax.broadcasted_iota(jnp.int32, (8, n), 0) == 7, x_ref[length - 8 :], 0.0)
    la, lb, _ = thirds(last)
    ends = contracted(la, la) + (contracted(lb, la) + contracted(la, lb))
    total_ref[...] = sums[:, :n] + length * cov
    previous_ref[...] = (sums[:, :n] - ends) + (length - 1) * cov
    lagged_ref[...] = sums[:, n:] + (length - 1) * drift_ref[...]
    count = shown_ref.shape[0]
    shown_ref[...] = x_ref[pl.ds(pl.multiple_of(place_ref[0] * count, count), count), :]


def scanned(core, place, own, other, ready, ft, kt, cov, length, parts):
    both, small, drift = ready
    n = ft.shape[0]
    square = jax.ShapeDtypeStruct((n, n), f32)
    vmem = pl.BlockSpec(memory_space=pltpu.VMEM)
    smem = pl.BlockSpec(memory_space=pltpu.SMEM)
    return pl.pallas_call(
        scan_kernel,
        out_shape=(
            jax.ShapeDtypeStruct((length, n), f32),
            jax.ShapeDtypeStruct((length // parts, n), f32),
            square, square, square,
        ),
        in_specs=[smem] * 2 + [vmem] * 8,
        out_specs=[vmem] * 5,
        scratch_shapes=[
            pltpu.VMEM((STEPS, length // STEPS, n), f32),
            pltpu.VMEM((STEPS, n, n), f32),
        ],
        compiler_params=pltpu.CompilerParams(vmem_limit_bytes=44 * 1024 * 1024),
        cost_estimate=pl.CostEstimate(flops=10**10, bytes_accessed=5 * 10**6, transcendentals=0),
        name="scan",
    )(core, place, own, other, both, small, ft, kt, cov, drift)


def swept(mats, n):
    row8 = lax.broadcasted_iota(jnp.int32, (8, n), 0)
    lane = lax.broadcasted_iota(jnp.int32, (1, n), 1)
    mats = [[m[8 * g : 8 * g + 8] for g in range(n // 8)] for m in mats]
    for k in range(n):
        found = []
        for m in mats:
            g, o = divmod(k, 8)
            pivot_row = m[g][o : o + 1, :]
            d = 1.0 / pivot_row[:, k : k + 1]
            s = jnp.where(lane == k, d, pivot_row * d)
            new = []
            for i, t in enumerate(m):
                u = jnp.where(lane == k, 0.0, t) - t[:, k : k + 1] * s
                new.append(jnp.where(row8 == o, s, u) if i == g else u)
            found.append(new)
        mats = found
    return [jnp.concatenate(m, axis=0) for m in mats]


def three(v, w):
    a, b, _ = thirds(v)
    c, d, _ = thirds(w)
    n = w.shape[1]
    y = plain(a, jnp.concatenate([c, d], axis=1))
    return y[:, :n] + (y[:, n:] + plain(b, c))


def inverse_kernel(total_ref, previous_ref, lagged_ref, cross_ref, loadings_ref, transition_ref, found_ref):
    n = total_ref.shape[0]
    eye = (
        lax.broadcasted_iota(jnp.int32, (n, n), 0) == lax.broadcasted_iota(jnp.int32, (n, n), 1)
    ).astype(f32)
    mats = [total_ref[...], previous_ref[...]]
    near, left = [], []
    for m in mats:
        bound = jnp.max(jnp.sum(jnp.abs(m), axis=0, keepdims=True), axis=1, keepdims=True)
        r = eye - m * (1.8 / bound)
        left.append(r)
        near.append((eye + r) * (1.8 / bound))
    for _ in range(SQUARINGS):
        for i in range(2):
            left[i] = three(left[i], left[i])
            near[i] = near[i] + three(near[i], left[i])
    size = jnp.zeros((1, 1), f32)
    for i in range(2):
        r = eye - high(mats[i], near[i])
        found_ref[i] = near[i] + three(near[i], r)
        square = jnp.sum(jnp.sum(r * r, axis=0, keepdims=True), axis=1, keepdims=True)
        size = jnp.maximum(size, square)

    @pl.when(jnp.logical_not(size[0, 0] < 1e-6))
    def _():
        one, two = swept([total_ref[...], previous_ref[...]], n)
        found_ref[0] = one
        found_ref[1] = two

    loadings_ref[...] = high(cross_ref[...], found_ref[0])
    transition_ref[...] = high(lagged_ref[...], found_ref[1])


def inverted(total, previous, lagged, cross):
    vmem = pl.BlockSpec(memory_space=pltpu.VMEM)
    square = jax.ShapeDtypeStruct(total.shape, f32)
    return pl.pallas_call(
        inverse_kernel,
        out_shape=(jax.ShapeDtypeStruct(cross.shape, f32), square),
        in_specs=[vmem] * 4,
        out_specs=[vmem] * 2,
        scratch_shapes=[pltpu.VMEM((2, *total.shape), f32)],
        compiler_params=pltpu.CompilerParams(vmem_limit_bytes=16 * 1024 * 1024),
        cost_estimate=pl.CostEstimate(flops=10**9, bytes_accessed=6 * 10**5, transcendentals=0),
        name="inverse",
    )(total, previous, lagged, cross)


def turned(value, axis, steps):
    count = lax.axis_size(axis)
    return lax.ppermute(value, axis, [(i, (i + steps) % count) for i in range(count)])


def over_z(value):
    count = lax.axis_size(Z)
    value = value + lax.ppermute(value, Z, [(i, i ^ 1) for i in range(count)])
    arrived = [turned(value, Z, 2 * k) for k in range(1, count // 2)]
    return sum(arrived, value)


def local(
    observations, loadings, noise_precision, transition, filter_cov, smoother_gain, smoothed_cov
):
    core = lax.axis_index(CORE)
    position = lax.axis_index(TM)
    length = observations.shape[0]
    width = transition.shape[0]
    half = length // 2
    groups = lax.axis_size((Y, X))
    rows = half // groups
    extra = width // groups
    weighted = noise_precision[:, None] * loadings
    scaled = weighted.astype(bf16)

    def projected(which):
        window = lax.dynamic_slice_in_dim(observations, which * half, half, 0)
        return jnp.dot(window, scaled, preferred_element_type=f32)

    info_part = jnp.dot(loadings.T, weighted, precision=precise, preferred_element_type=f32)
    info_part = info_part + turned(info_part, CORE, 1)
    mine = projected(core) + turned(projected(1 - core), CORE, 1)
    pieces = jnp.concatenate(
        [mine.reshape(groups, rows, width), info_part.reshape(groups, extra, width)], axis=1
    )
    arrived = lax.all_to_all(pieces, (Y, X), split_axis=0, concat_axis=0, tiled=True)
    block = over_z(arrived.sum(axis=0))
    copies = jnp.broadcast_to(block, (groups, *block.shape))
    own = lax.all_to_all(copies, (Y, X), split_axis=0, concat_axis=0, tiled=True)
    other = turned(own, CORE, 1)
    ready = readied(transition.T, filter_cov.T, smoother_gain.T, smoothed_cov, length)
    smoothed, shown, total, previous, lagged = scanned(
        core[None].astype(jnp.int32), position[None].astype(jnp.int32), own, other, ready,
        transition.T, filter_cov.T, smoothed_cov, length, lax.axis_size(TM),
    )
    cross = jnp.einsum(
        "ts,tk->sk", observations, smoothed.astype(bf16), preferred_element_type=f32
    )
    new_loadings, new_transition = inverted(total, previous, lagged, cross)
    return (shown, new_loadings, new_transition)


def solution(mesh):
    split = Mesh(mesh.devices.reshape(4, 4, 2, mesh.shape["sr"]), (Y, X, CORE, Z))
    in_specs = (P(None, SR_TM), P(SR_TM, None), P(SR_TM), P(), P(), P(), P())
    out_specs = (P(TM, None), P(SR_TM, None), P())
    return jax.shard_map(local, mesh=split, in_specs=in_specs, out_specs=out_specs, check_vma=False)
```

```python
import jax
import jax.numpy as jnp
from jax import lax
from jax.experimental import pallas as pl
from jax.experimental.pallas import tpu as pltpu
from jax.sharding import Mesh
from jax.sharding import PartitionSpec as P

Y, X, CORE, Z = "tm_0", "tm_1", "tm_2", "sr"
TM = (Y, X, CORE)
SR_TM = (Z, Y, X, CORE)

STEPS = 8
SQUARINGS = 7
FIRST = 4
f32 = jnp.float32
bf16 = jnp.bfloat16
precise = lax.Precision.HIGHEST


def thirds(v):
    a = v.astype(bf16)
    rest = v - a.astype(f32)
    b = rest.astype(bf16)
    c = (rest - b.astype(f32)).astype(bf16)
    return a, b, c


def right(w):
    a, b, c = thirds(w)
    both = jnp.concatenate([a, b], axis=1)
    if w.shape[0] <= 128:
        return both, (jnp.concatenate([c, a], axis=0),)
    return both, (c, a)


def plain(a, b):
    return jnp.dot(a, b, preferred_element_type=f32)


def times(v, w):
    return times_split(thirds(v), w)


def times_split(v, w):
    both, small = w
    n = both.shape[1] // 2
    a, b, c = v
    p, q = plain(a, both), plain(b, both)
    if len(small) == 1:
        least = plain(jnp.concatenate([a, c], axis=1), small[0])
    else:
        least = plain(a, small[0]) + plain(c, small[1])
    return p[:, :n] + (p[:, n:] + q[:, :n] + (q[:, n:] + least))


def high(a, b):
    return times(a, right(b))


def contracted(a, b):
    return lax.dot_general(a, b, (((0,), (0,)), ((), ())), preferred_element_type=f32)


def moved(v, shift, row):
    n = v.shape[0]
    keep = (row >= shift) if shift > 0 else (row < n + shift)
    return jnp.where(keep, pltpu.roll(v, shift % n, 0), 0.0)


def powers(a, n):
    found = [a]
    while len(found) < STEPS:
        more = high(jnp.concatenate(found, axis=0), found[-1])
        found = found + [more[i * n : (i + 1) * n] for i in range(len(found))]
    return found


def kept(blocks_at, count=1):
    both = blocks_at[0]
    small = blocks_at[1]
    if count == 1:
        return both, (jnp.concatenate([small, both[:, : both.shape[1] // 2]], axis=0),)
    return both, (small, both[:, : both.shape[1] // 2])


def beneath(*pieces):
    return tuple(jnp.concatenate(p, axis=0) for p in zip(*pieces))


def pieces_of(w):
    a, b, c = thirds(w)
    return jnp.concatenate([a, b], axis=1), c


def ready_kernel(ft_ref, kt_ref, jt_ref, cov_ref, both_ref, small_ref, drift_ref):
    n = ft_ref.shape[0]
    ft, kt, jt = ft_ref[...], kt_ref[...], jt_ref[...]
    eye = (
        lax.broadcasted_iota(jnp.int32, (n, n), 0) == lax.broadcasted_iota(jnp.int32, (n, n), 1)
    ).astype(f32)

    def put(at, w):
        both, small = pieces_of(w)
        both_ref[at] = both
        small_ref[at] = small

    put(0, kt)
    put(1, eye - high(ft, jt))
    raised = powers(jt, n)
    put(2, ft)
    put(3, high(ft, raised[-1]))
    for k, w in enumerate(raised):
        put(FIRST + k, w)
    power = raised[-1]
    for k in range(FIRST + STEPS, both_ref.shape[0]):
        power = high(power, power)
        put(k, power)
    drift_ref[...] = high(cov_ref[...], jt)


def readied(ft, kt, jt, cov, length):
    n = ft.shape[0]
    count = FIRST + STEPS + (length // STEPS).bit_length() - 2
    vmem = pl.BlockSpec(memory_space=pltpu.VMEM)
    return pl.pallas_call(
        ready_kernel,
        out_shape=(
            jax.ShapeDtypeStruct((count, n, 2 * n), bf16),
            jax.ShapeDtypeStruct((count, n, n), bf16),
            jax.ShapeDtypeStruct((n, n), f32),
        ),
        in_specs=[vmem] * 4,
        out_specs=[vmem] * 3,
        compiler_params=pltpu.CompilerParams(vmem_limit_bytes=16 * 1024 * 1024),
        cost_estimate=pl.CostEstimate(flops=10**9, bytes_accessed=2 * 10**6, transcendentals=0),
        name="ready",
    )(ft, kt, jt, cov)


def scan_kernel(
    core_ref, place_ref, own_ref, other_ref, both_ref, small_ref, ft_ref, cov_ref, drift_ref,
    x_ref, shown_ref, total_ref, previous_ref, lagged_ref, loc_ref, mat_ref,
):
    n = ft_ref.shape[0]
    groups = own_ref.shape[0]
    length = x_ref.shape[0]
    rows = length // (2 * groups)
    blocks = length // STEPS
    first = core_ref[0] == 0
    cov = cov_ref[...]
    held = lambda k: (both_ref[k], small_ref[k])
    info = jnp.concatenate([own_ref[g, rows:] + other_ref[g, rows:] for g in range(groups)], axis=0)
    row = lax.broadcasted_iota(jnp.int32, (blocks, n), 0)
    levels = blocks.bit_length() - 1
    a = ft_ref[...] - times(high(ft_ref[...], info), kept(held(0)))

    def drive(j):
        def half(ref):
            parts = [ref[g, pl.ds(j, rows // STEPS, stride=STEPS), :] for g in range(groups)]
            return jnp.concatenate(parts, axis=0)

        own, other = half(own_ref), half(other_ref)
        return jnp.concatenate(
            [jnp.where(first, own, other), jnp.where(first, other, own)], axis=0
        )

    apow, leaps = [a], []
    step = kept(beneath(pieces_of(a), held(0)), 2)
    state = times(drive(0), kept(held(0)))
    loc_ref[0] = state
    for j in range(1, STEPS):
        state = times(jnp.concatenate([state, drive(j)], axis=1), step)
        loc_ref[j] = state
        if len(apow) < STEPS:
            more = high(jnp.concatenate(apow, axis=0), apow[-1])
            apow = apow + [more[i * n : (i + 1) * n] for i in range(len(apow))]
            if len(apow) == STEPS:
                leap = apow[-1]
                leaps.append(right(leap))
        elif len(leaps) < levels:
            leap = times(leap, leaps[-1])
            leaps.append(right(leap))
    enter = state
    level = 0
    back = kept(beneath(held(FIRST), held(1)), 2)
    both = lambda j: jnp.concatenate([loc_ref[j], apow[j]], axis=0)
    out = times(both(STEPS - 1), kept(held(1)))
    for j in range(STEPS - 1, -1, -1):
        if j < STEPS - 1:
            out = times(jnp.concatenate([out, both(j)], axis=1), back)
        loc_ref[j] = out[:blocks]
        mat_ref[j] = out[blocks:]
        if level < levels:
            if len(leaps) < levels:
                leap = times(leap, leaps[-1])
                leaps.append(right(leap))
            enter = enter + times(moved(enter, 1 << level, row), leaps[level])
            level += 1
    while level < levels:
        if len(leaps) < levels:
            leap = times(leap, leaps[-1])
            leaps.append(right(leap))
        enter = enter + times(moved(enter, 1 << level, row), leaps[level])
        level += 1
    e = moved(enter, 1, row)
    tail = lax.broadcasted_iota(jnp.int32, (8, n), 0) == 7
    final = jnp.where(tail, enter[blocks - 8 :], 0.0)
    after = times(final, kept(held(2)))
    z = loc_ref[0] + high(e, mat_ref[0])
    z = jnp.concatenate([z[: blocks - 8], z[blocks - 8 :] + times(final, kept(held(3)))], axis=0)
    for level in range(levels):
        z = z + times(moved(z, -(1 << level), row), kept(held(FIRST + STEPS - 1 + level)))
    coming = moved(z, -1, row)
    coming = jnp.concatenate([coming[: blocks - 8], coming[blocks - 8 :] + after], axis=0)
    mixed = thirds(jnp.concatenate([e, coming], axis=1))
    sums = jnp.zeros((n, 2 * n), f32)

    def outer(x, prior):
        xa, xb = x
        pa, pb = prior
        pair = jnp.concatenate([xa, pa], axis=1)
        rest = jnp.concatenate([xb, pb], axis=1)
        return contracted(xa, pair) + (contracted(xb, pair) + contracted(xa, rest))

    opening = prior = thirds(z)[:2]
    x_ref[pl.ds(0, blocks, stride=STEPS), :] = z
    for j in range(1, STEPS):
        w = kept(beneath(pieces_of(mat_ref[j]), held(FIRST + STEPS - 1 - j)), 2)
        x = loc_ref[j] + times_split(mixed, w)
        x_ref[pl.ds(j, blocks, stride=STEPS), :] = x
        here = thirds(x)[:2]
        sums = sums + outer(here, prior)
        prior = here
    sums = sums + outer(opening, thirds(moved(x, 1, row))[:2])
    last = jnp.where(tail, x_ref[length - 8 :], 0.0)
    la, lb, _ = thirds(last)
    ends = contracted(la, la) + (contracted(lb, la) + contracted(la, lb))
    total_ref[...] = sums[:, :n] + length * cov
    previous_ref[...] = (sums[:, :n] - ends) + (length - 1) * cov
    lagged_ref[...] = sums[:, n:] + (length - 1) * drift_ref[...]
    count = shown_ref.shape[0]
    shown_ref[...] = x_ref[pl.ds(pl.multiple_of(place_ref[0] * count, count), count), :]


def scanned(core, place, own, other, ready, ft, cov, length, parts):
    both, small, drift = ready
    n = ft.shape[0]
    square = jax.ShapeDtypeStruct((n, n), f32)
    vmem = pl.BlockSpec(memory_space=pltpu.VMEM)
    smem = pl.BlockSpec(memory_space=pltpu.SMEM)
    return pl.pallas_call(
        scan_kernel,
        out_shape=(
            jax.ShapeDtypeStruct((length, n), f32),
            jax.ShapeDtypeStruct((length // parts, n), f32),
            square, square, square,
        ),
        in_specs=[smem] * 2 + [vmem] * 7,
        out_specs=[vmem] * 5,
        scratch_shapes=[
            pltpu.VMEM((STEPS, length // STEPS, n), f32),
            pltpu.VMEM((STEPS, n, n), f32),
        ],
        compiler_params=pltpu.CompilerParams(vmem_limit_bytes=44 * 1024 * 1024),
        cost_estimate=pl.CostEstimate(flops=10**10, bytes_accessed=5 * 10**6, transcendentals=0),
        name="scan",
    )(core, place, own, other, both, small, ft, cov, drift)


def swept(mats, n):
    row8 = lax.broadcasted_iota(jnp.int32, (8, n), 0)
    lane = lax.broadcasted_iota(jnp.int32, (1, n), 1)
    mats = [[m[8 * g : 8 * g + 8] for g in range(n // 8)] for m in mats]
    for k in range(n):
        found = []
        for m in mats:
            g, o = divmod(k, 8)
            pivot_row = m[g][o : o + 1, :]
            d = 1.0 / pivot_row[:, k : k + 1]
            s = jnp.where(lane == k, d, pivot_row * d)
            new = []
            for i, t in enumerate(m):
                u = jnp.where(lane == k, 0.0, t) - t[:, k : k + 1] * s
                new.append(jnp.where(row8 == o, s, u) if i == g else u)
            found.append(new)
        mats = found
    return [jnp.concatenate(m, axis=0) for m in mats]


def three(v, w):
    a, b, _ = thirds(v)
    c, d, _ = thirds(w)
    n = w.shape[1]
    y = plain(a, jnp.concatenate([c, d], axis=1))
    return y[:, :n] + (y[:, n:] + plain(b, c))


def inverse_kernel(total_ref, previous_ref, lagged_ref, cross_ref, loadings_ref, transition_ref, found_ref):
    n = total_ref.shape[0]
    eye = (
        lax.broadcasted_iota(jnp.int32, (n, n), 0) == lax.broadcasted_iota(jnp.int32, (n, n), 1)
    ).astype(f32)
    mats = [total_ref[...], previous_ref[...]]
    near, left = [], []
    for m in mats:
        bound = jnp.max(jnp.sum(jnp.abs(m), axis=0, keepdims=True), axis=1, keepdims=True)
        r = eye - m * (1.8 / bound)
        left.append(r)
        near.append((eye + r) * (1.8 / bound))
    for _ in range(SQUARINGS):
        for i in range(2):
            left[i] = three(left[i], left[i])
            near[i] = near[i] + three(near[i], left[i])
    size = jnp.zeros((1, 1), f32)
    for i in range(2):
        r = eye - high(mats[i], near[i])
        found_ref[i] = near[i] + three(near[i], r)
        square = jnp.sum(jnp.sum(r * r, axis=0, keepdims=True), axis=1, keepdims=True)
        size = jnp.maximum(size, square)

    @pl.when(jnp.logical_not(size[0, 0] < 1e-6))
    def _():
        one, two = swept([total_ref[...], previous_ref[...]], n)
        found_ref[0] = one
        found_ref[1] = two

    loadings_ref[...] = high(cross_ref[...], found_ref[0])
    transition_ref[...] = high(lagged_ref[...], found_ref[1])


def inverted(total, previous, lagged, cross):
    vmem = pl.BlockSpec(memory_space=pltpu.VMEM)
    square = jax.ShapeDtypeStruct(total.shape, f32)
    return pl.pallas_call(
        inverse_kernel,
        out_shape=(jax.ShapeDtypeStruct(cross.shape, f32), square),
        in_specs=[vmem] * 4,
        out_specs=[vmem] * 2,
        scratch_shapes=[pltpu.VMEM((2, *total.shape), f32)],
        compiler_params=pltpu.CompilerParams(vmem_limit_bytes=16 * 1024 * 1024),
        cost_estimate=pl.CostEstimate(flops=10**9, bytes_accessed=6 * 10**5, transcendentals=0),
        name="inverse",
    )(total, previous, lagged, cross)


CHUNKS = 4


def scaled_by(loadings, noise_row):
    count, n = loadings.shape
    noise = jnp.transpose(jnp.broadcast_to(noise_row, (n, count)))
    return noise * loadings


def project_kernel(start_ref, observations_ref, loadings_ref, noise_ref, out_ref, *rest):
    window_ref, sem = rest[-2:]
    chunk = out_ref.shape[0] // CHUNKS
    start = pl.multiple_of(start_ref[0], out_ref.shape[0])

    def copy(k):
        rows = pl.ds(k * chunk, chunk)
        there = pl.ds(start + k * chunk, chunk)
        return pltpu.make_async_copy(
            observations_ref.at[there, :], window_ref.at[rows, :], sem.at[k]
        )

    for k in range(CHUNKS):
        copy(k).start()
    loadings = loadings_ref[...]
    weighted = scaled_by(loadings, noise_ref[...])
    scaled = weighted.astype(bf16)
    if len(rest) == 3:
        a, b, c = thirds(loadings)
        p, q, r = thirds(weighted)
        pair = contracted(a, jnp.concatenate([p, q], axis=1))
        other = contracted(b, jnp.concatenate([p, q], axis=1))
        n = loadings.shape[1]
        least = contracted(a, r) + contracted(c, p)
        rest[0][...] = pair[:, :n] + (pair[:, n:] + other[:, :n] + (other[:, n:] + least))
    for k in range(CHUNKS):
        copy(k).wait()
        rows = pl.ds(k * chunk, chunk)
        out_ref[rows, :] = plain(window_ref[rows, :], scaled)


def projected(observations, loadings, noise, start, with_info):
    half, n = observations.shape[0] // 2, loadings.shape[1]
    vmem = pl.BlockSpec(memory_space=pltpu.VMEM)
    shapes = [jax.ShapeDtypeStruct((half, n), f32), jax.ShapeDtypeStruct((n, n), f32)]
    count = 2 if with_info else 1
    return pl.pallas_call(
        project_kernel,
        out_shape=tuple(shapes[:count]),
        in_specs=[
            pl.BlockSpec(memory_space=pltpu.SMEM), pl.BlockSpec(memory_space=pltpu.HBM), vmem, vmem
        ],
        out_specs=tuple([vmem] * count),
        scratch_shapes=[
            pltpu.VMEM((half, observations.shape[1]), bf16),
            pltpu.SemaphoreType.DMA((CHUNKS,)),
        ],
        compiler_params=pltpu.CompilerParams(vmem_limit_bytes=62 * 1024 * 1024),
        cost_estimate=pl.CostEstimate(flops=10**8, bytes_accessed=3 * 10**6, transcendentals=0),
        name="project",
    )(start[None].astype(jnp.int32), observations, loadings, noise[None, :])


def turned(value, axis, steps):
    count = lax.axis_size(axis)
    return lax.ppermute(value, axis, [(i, (i + steps) % count) for i in range(count)])


def over_z(value):
    count = lax.axis_size(Z)
    value = value + lax.ppermute(value, Z, [(i, i ^ 1) for i in range(count)])
    arrived = [turned(value, Z, k) for k in (2, count - 2, 4)]
    return sum(arrived, value)


def local(
    observations, loadings, noise_precision, transition, filter_cov, smoother_gain, smoothed_cov
):
    core = lax.axis_index(CORE)
    position = lax.axis_index(TM)
    length = observations.shape[0]
    width = transition.shape[0]
    half = length // 2
    groups = lax.axis_size((Y, X))
    rows = half // groups
    extra = width // groups
    (given,) = projected(observations, loadings, noise_precision, (1 - core) * half, False)
    taken = turned(given, CORE, 1)
    mine, info_part = projected(observations, loadings, noise_precision, core * half, True)
    mine = mine + taken
    pieces = jnp.concatenate(
        [mine.reshape(groups, rows, width), info_part.reshape(groups, extra, width)], axis=1
    )
    arrived = lax.all_to_all(pieces, (Y, X), split_axis=0, concat_axis=0, tiled=True)
    block = over_z(arrived.sum(axis=0))
    copies = jnp.broadcast_to(block, (groups, *block.shape))
    own = lax.all_to_all(copies, (Y, X), split_axis=0, concat_axis=0, tiled=True)
    other = turned(own, CORE, 1)
    ready = readied(transition.T, filter_cov.T, smoother_gain.T, smoothed_cov, length)
    smoothed, shown, total, previous, lagged = scanned(
        core[None].astype(jnp.int32), position[None].astype(jnp.int32), own, other, ready,
        transition.T, smoothed_cov, length, lax.axis_size(TM),
    )
    cross = jnp.einsum(
        "ts,tk->sk", observations, smoothed.astype(bf16), preferred_element_type=f32
    )
    new_loadings, new_transition = inverted(total, previous, lagged, cross)
    return (shown, new_loadings, new_transition)


def solution(mesh):
    split = Mesh(mesh.devices.reshape(4, 4, 2, mesh.shape["sr"]), (Y, X, CORE, Z))
    in_specs = (P(None, SR_TM), P(SR_TM, None), P(SR_TM), P(), P(), P(), P())
    out_specs = (P(TM, None), P(SR_TM, None), P())
    return jax.shard_map(local, mesh=split, in_specs=in_specs, out_specs=out_specs, check_vma=False)
```

```python
import jax
import jax.numpy as jnp
from jax import lax
from jax.experimental.layout import Layout, with_layout_constraint
from jax.experimental import pallas as pl
from jax.experimental.pallas import tpu as pltpu
from jax.sharding import Mesh
from jax.sharding import PartitionSpec as P

Y, X, CORE, Z = "tm_0", "tm_1", "tm_2", "sr"
TM = (Y, X, CORE)
SR_TM = (Z, Y, X, CORE)

STEPS = 8
SQUARINGS = 7
FIRST = 4
f32 = jnp.float32
bf16 = jnp.bfloat16
precise = lax.Precision.HIGHEST


def thirds(v):
    a = v.astype(bf16)
    rest = v - a.astype(f32)
    b = rest.astype(bf16)
    c = (rest - b.astype(f32)).astype(bf16)
    return a, b, c


def right(w):
    a, b, c = thirds(w)
    both = jnp.concatenate([a, b], axis=1)
    if w.shape[0] <= 128:
        return both, (jnp.concatenate([c, a], axis=0),)
    return both, (c, a)


def plain(a, b):
    return jnp.dot(a, b, preferred_element_type=f32)


def times(v, w):
    return times_split(thirds(v), w)


def times_split(v, w):
    both, small = w
    n = both.shape[1] // 2
    a, b, c = v
    p, q = plain(a, both), plain(b, both)
    if len(small) == 1:
        least = plain(jnp.concatenate([a, c], axis=1), small[0])
    else:
        least = plain(a, small[0]) + plain(c, small[1])
    return p[:, :n] + (p[:, n:] + q[:, :n] + (q[:, n:] + least))


def high(a, b):
    return times(a, right(b))


def contracted(a, b):
    return lax.dot_general(a, b, (((0,), (0,)), ((), ())), preferred_element_type=f32)


def moved(v, shift, row):
    n = v.shape[0]
    keep = (row >= shift) if shift > 0 else (row < n + shift)
    return jnp.where(keep, pltpu.roll(v, shift % n, 0), 0.0)


def powers(a, n):
    found = [a]
    while len(found) < STEPS:
        more = high(jnp.concatenate(found, axis=0), found[-1])
        found = found + [more[i * n : (i + 1) * n] for i in range(len(found))]
    return found


def kept(blocks_at, count=1):
    both = blocks_at[0]
    small = blocks_at[1]
    if count == 1:
        return both, (jnp.concatenate([small, both[:, : both.shape[1] // 2]], axis=0),)
    return both, (small, both[:, : both.shape[1] // 2])


def beneath(*pieces):
    return tuple(jnp.concatenate(p, axis=0) for p in zip(*pieces))


def pieces_of(w):
    a, b, c = thirds(w)
    return jnp.concatenate([a, b], axis=1), c


def ready_kernel(ft_ref, kt_ref, jt_ref, cov_ref, both_ref, small_ref, drift_ref):
    n = ft_ref.shape[0]
    ft, kt, jt = ft_ref[...], kt_ref[...], jt_ref[...]
    eye = (
        lax.broadcasted_iota(jnp.int32, (n, n), 0) == lax.broadcasted_iota(jnp.int32, (n, n), 1)
    ).astype(f32)

    def put(at, w):
        both, small = pieces_of(w)
        both_ref[at] = both
        small_ref[at] = small

    put(0, kt)
    put(1, eye - high(ft, jt))
    raised = powers(jt, n)
    put(2, ft)
    put(3, high(ft, raised[-1]))
    for k, w in enumerate(raised):
        put(FIRST + k, w)
    power = raised[-1]
    for k in range(FIRST + STEPS, both_ref.shape[0]):
        power = high(power, power)
        put(k, power)
    drift_ref[...] = high(cov_ref[...], jt)


def readied(ft, kt, jt, cov, length):
    n = ft.shape[0]
    count = FIRST + STEPS + (length // STEPS).bit_length() - 2
    vmem = pl.BlockSpec(memory_space=pltpu.VMEM)
    return pl.pallas_call(
        ready_kernel,
        out_shape=(
            jax.ShapeDtypeStruct((count, n, 2 * n), bf16),
            jax.ShapeDtypeStruct((count, n, n), bf16),
            jax.ShapeDtypeStruct((n, n), f32),
        ),
        in_specs=[vmem] * 4,
        out_specs=[vmem] * 3,
        compiler_params=pltpu.CompilerParams(vmem_limit_bytes=16 * 1024 * 1024),
        cost_estimate=pl.CostEstimate(flops=10**9, bytes_accessed=2 * 10**6, transcendentals=0),
        name="ready",
    )(ft, kt, jt, cov)


def begin_kernel(own_ref, kt_ref, ft_ref, power_ref):
    n = ft_ref.shape[0]
    groups = own_ref.shape[0]
    rows = own_ref.shape[1] - n // groups
    info = jnp.concatenate([own_ref[g, rows:] for g in range(groups)], axis=0)
    ft = ft_ref[...]
    a = ft - high(high(ft, info), kt_ref[...])
    for k, w in enumerate(powers(a, n)):
        power_ref[k] = w


def begun(own, kt, ft):
    n = ft.shape[0]
    vmem = pl.BlockSpec(memory_space=pltpu.VMEM)
    return pl.pallas_call(
        begin_kernel,
        out_shape=jax.ShapeDtypeStruct((STEPS, n, n), f32),
        in_specs=[vmem] * 3,
        out_specs=vmem,
        compiler_params=pltpu.CompilerParams(vmem_limit_bytes=16 * 1024 * 1024),
        cost_estimate=pl.CostEstimate(flops=10**9, bytes_accessed=2 * 10**6, transcendentals=0),
        name="begin",
    )(own, kt, ft)


def scan_kernel(
    core_ref, place_ref, own_ref, other_ref, both_ref, small_ref, power_ref, cov_ref, drift_ref,
    x_ref, shown_ref, total_ref, previous_ref, lagged_ref, loc_ref, mat_ref,
):
    n = cov_ref.shape[0]
    groups = own_ref.shape[0]
    length = x_ref.shape[0]
    rows = length // (2 * groups)
    blocks = length // STEPS
    first = core_ref[0] == 0
    cov = cov_ref[...]
    held = lambda k: (both_ref[k], small_ref[k])
    row = lax.broadcasted_iota(jnp.int32, (blocks, n), 0)
    levels = blocks.bit_length() - 1
    apow = [power_ref[k] for k in range(STEPS)]
    a = apow[0]
    leap = apow[-1]
    leaps = [right(leap)]

    def drive(j):
        def half(ref):
            parts = [ref[g, pl.ds(j, rows // STEPS, stride=STEPS), :] for g in range(groups)]
            return jnp.concatenate(parts, axis=0)

        own, other = half(own_ref), half(other_ref)
        return jnp.concatenate(
            [jnp.where(first, own, other), jnp.where(first, other, own)], axis=0
        )

    step = kept(beneath(pieces_of(a), held(0)), 2)
    state = times(drive(0), kept(held(0)))
    loc_ref[0] = state
    for j in range(1, STEPS):
        state = times(jnp.concatenate([state, drive(j)], axis=1), step)
        loc_ref[j] = state
        if len(leaps) < levels:
            leap = times(leap, leaps[-1])
            leaps.append(right(leap))
    enter = state
    level = 0
    back = kept(beneath(held(FIRST), held(1)), 2)
    both = lambda j: jnp.concatenate([loc_ref[j], apow[j]], axis=0)
    out = times(both(STEPS - 1), kept(held(1)))
    for j in range(STEPS - 1, -1, -1):
        if j < STEPS - 1:
            out = times(jnp.concatenate([out, both(j)], axis=1), back)
        loc_ref[j] = out[:blocks]
        mat_ref[j] = out[blocks:]
        if level < levels:
            if len(leaps) < levels:
                leap = times(leap, leaps[-1])
                leaps.append(right(leap))
            enter = enter + times(moved(enter, 1 << level, row), leaps[level])
            level += 1
    while level < levels:
        if len(leaps) < levels:
            leap = times(leap, leaps[-1])
            leaps.append(right(leap))
        enter = enter + times(moved(enter, 1 << level, row), leaps[level])
        level += 1
    e = moved(enter, 1, row)
    tail = lax.broadcasted_iota(jnp.int32, (8, n), 0) == 7
    final = jnp.where(tail, enter[blocks - 8 :], 0.0)
    after = times(final, kept(held(2)))
    z = loc_ref[0] + high(e, mat_ref[0])
    z = jnp.concatenate([z[: blocks - 8], z[blocks - 8 :] + times(final, kept(held(3)))], axis=0)
    for level in range(levels):
        z = z + times(moved(z, -(1 << level), row), kept(held(FIRST + STEPS - 1 + level)))
    coming = moved(z, -1, row)
    coming = jnp.concatenate([coming[: blocks - 8], coming[blocks - 8 :] + after], axis=0)
    mixed = thirds(jnp.concatenate([e, coming], axis=1))
    sums = jnp.zeros((n, 2 * n), f32)

    def outer(x, prior):
        xa, xb = x
        pa, pb = prior
        pair = jnp.concatenate([xa, pa], axis=1)
        rest = jnp.concatenate([xb, pb], axis=1)
        return contracted(xa, pair) + (contracted(xb, pair) + contracted(xa, rest))

    opening = prior = thirds(z)[:2]
    x_ref[pl.ds(0, blocks, stride=STEPS), :] = z
    for j in range(1, STEPS):
        w = kept(beneath(pieces_of(mat_ref[j]), held(FIRST + STEPS - 1 - j)), 2)
        x = loc_ref[j] + times_split(mixed, w)
        x_ref[pl.ds(j, blocks, stride=STEPS), :] = x
        here = thirds(x)[:2]
        sums = sums + outer(here, prior)
        prior = here
    sums = sums + outer(opening, thirds(moved(x, 1, row))[:2])
    last = jnp.where(tail, x_ref[length - 8 :], 0.0)
    la, lb, _ = thirds(last)
    ends = contracted(la, la) + (contracted(lb, la) + contracted(la, lb))
    total_ref[...] = sums[:, :n] + length * cov
    previous_ref[...] = (sums[:, :n] - ends) + (length - 1) * cov
    lagged_ref[...] = sums[:, n:] + (length - 1) * drift_ref[...]
    count = shown_ref.shape[0]
    shown_ref[...] = x_ref[pl.ds(pl.multiple_of(place_ref[0] * count, count), count), :]


def scanned(core, place, own, other, ready, power, cov, length, parts):
    both, small, drift = ready
    n = cov.shape[0]
    square = jax.ShapeDtypeStruct((n, n), f32)
    vmem = pl.BlockSpec(memory_space=pltpu.VMEM)
    smem = pl.BlockSpec(memory_space=pltpu.SMEM)
    return pl.pallas_call(
        scan_kernel,
        out_shape=(
            jax.ShapeDtypeStruct((length, n), f32),
            jax.ShapeDtypeStruct((length // parts, n), f32),
            square, square, square,
        ),
        in_specs=[smem] * 2 + [vmem] * 7,
        out_specs=[vmem] * 5,
        scratch_shapes=[
            pltpu.VMEM((STEPS, length // STEPS, n), f32),
            pltpu.VMEM((STEPS, n, n), f32),
        ],
        compiler_params=pltpu.CompilerParams(vmem_limit_bytes=44 * 1024 * 1024),
        cost_estimate=pl.CostEstimate(flops=10**10, bytes_accessed=5 * 10**6, transcendentals=0),
        name="scan",
    )(core, place, own, other, both, small, power, cov, drift)


def swept(mats, n):
    row8 = lax.broadcasted_iota(jnp.int32, (8, n), 0)
    lane = lax.broadcasted_iota(jnp.int32, (1, n), 1)
    mats = [[m[8 * g : 8 * g + 8] for g in range(n // 8)] for m in mats]
    for k in range(n):
        found = []
        for m in mats:
            g, o = divmod(k, 8)
            pivot_row = m[g][o : o + 1, :]
            d = 1.0 / pivot_row[:, k : k + 1]
            s = jnp.where(lane == k, d, pivot_row * d)
            new = []
            for i, t in enumerate(m):
                u = jnp.where(lane == k, 0.0, t) - t[:, k : k + 1] * s
                new.append(jnp.where(row8 == o, s, u) if i == g else u)
            found.append(new)
        mats = found
    return [jnp.concatenate(m, axis=0) for m in mats]


def three(v, w):
    a, b, _ = thirds(v)
    c, d, _ = thirds(w)
    n = w.shape[1]
    y = plain(a, jnp.concatenate([c, d], axis=1))
    return y[:, :n] + (y[:, n:] + plain(b, c))


def inverse_kernel(total_ref, previous_ref, lagged_ref, cross_ref, loadings_ref, transition_ref):
    n = total_ref.shape[0]
    eye = (
        lax.broadcasted_iota(jnp.int32, (n, n), 0) == lax.broadcasted_iota(jnp.int32, (n, n), 1)
    ).astype(f32)
    mats = [total_ref[...], previous_ref[...]]
    near, left = [], []
    for m in mats:
        bound = jnp.max(jnp.sum(jnp.abs(m), axis=0, keepdims=True), axis=1, keepdims=True)
        r = eye - m * (1.8 / bound)
        left.append(r)
        near.append((eye + r) * (1.8 / bound))
    for _ in range(SQUARINGS):
        for i in range(2):
            left[i] = three(left[i], left[i])
            near[i] = near[i] + three(near[i], left[i])
    size = jnp.zeros((1, 1), f32)
    for i, (taken_ref, out_ref) in enumerate(
        ((cross_ref, loadings_ref), (lagged_ref, transition_ref))
    ):
        w = right(near[i])
        r = eye - times(mats[i], w)
        first = times(taken_ref[...], w)
        out_ref[...] = first + three(first, r)
        square = jnp.sum(jnp.sum(r * r, axis=0, keepdims=True), axis=1, keepdims=True)
        size = jnp.maximum(size, square)

    @pl.when(jnp.logical_not(size[0, 0] < 1e-6))
    def _():
        one, two = swept([total_ref[...], previous_ref[...]], n)
        loadings_ref[...] = high(cross_ref[...], one)
        transition_ref[...] = high(lagged_ref[...], two)


def inverted(total, previous, lagged, cross):
    vmem = pl.BlockSpec(memory_space=pltpu.VMEM)
    square = jax.ShapeDtypeStruct(total.shape, f32)
    return pl.pallas_call(
        inverse_kernel,
        out_shape=(jax.ShapeDtypeStruct(cross.shape, f32), square),
        in_specs=[vmem] * 4,
        out_specs=[vmem] * 2,
        compiler_params=pltpu.CompilerParams(vmem_limit_bytes=16 * 1024 * 1024),
        cost_estimate=pl.CostEstimate(flops=10**9, bytes_accessed=6 * 10**5, transcendentals=0),
        name="inverse",
    )(total, previous, lagged, cross)


def turned(value, axis, steps):
    count = lax.axis_size(axis)
    return lax.ppermute(value, axis, [(i, (i + steps) % count) for i in range(count)])


def over_z(value):
    count = lax.axis_size(Z)
    value = value + lax.ppermute(value, Z, [(i, i ^ 1) for i in range(count)])
    arrived = [turned(value, Z, 2 * k) for k in range(1, count // 2)]
    return sum(arrived, value)


def local(
    observations, loadings, noise_precision, transition, filter_cov, smoother_gain, smoothed_cov
):
    core = lax.axis_index(CORE)
    position = lax.axis_index(TM)
    length = observations.shape[0]
    width = transition.shape[0]
    half = length // 2
    groups = lax.axis_size((Y, X))
    rows = half // groups
    extra = width // groups
    weighted = noise_precision[:, None] * loadings
    scaled = weighted.astype(bf16)

    info_part = jnp.dot(loadings.T, weighted, precision=precise, preferred_element_type=f32)
    info_part = info_part + turned(info_part, CORE, 1)
    whole = jnp.dot(observations, scaled, preferred_element_type=f32)
    whole = with_layout_constraint(whole, Layout(major_to_minor=(0, 1)))
    given = lax.dynamic_slice_in_dim(whole, (1 - core) * half, half, 0)
    mine = lax.dynamic_slice_in_dim(whole, core * half, half, 0)
    given, mine = lax.optimization_barrier((given, mine))
    mine = mine + turned(given, CORE, 1)
    pieces = jnp.concatenate(
        [mine.reshape(groups, rows, width), info_part.reshape(groups, extra, width)], axis=1
    )
    arrived = lax.all_to_all(pieces, (Y, X), split_axis=0, concat_axis=0, tiled=True)
    block = over_z(arrived.sum(axis=0))
    ready = readied(transition.T, filter_cov.T, smoother_gain.T, smoothed_cov, length)
    block, ready = lax.optimization_barrier((block, ready))
    copies = jnp.broadcast_to(block, (groups, *block.shape))
    own = lax.all_to_all(copies, (Y, X), split_axis=0, concat_axis=0, tiled=True)
    other = turned(own, CORE, 1)
    power = begun(own, filter_cov.T, transition.T)
    smoothed, shown, total, previous, lagged = scanned(
        core[None].astype(jnp.int32), position[None].astype(jnp.int32), own, other, ready,
        power, smoothed_cov, length, lax.axis_size(TM),
    )
    cross = jnp.einsum(
        "ts,tk->sk", observations, smoothed.astype(bf16), preferred_element_type=f32
    )
    new_loadings, new_transition = inverted(total, previous, lagged, cross)
    return (shown, new_loadings, new_transition)


def solution(mesh):
    split = Mesh(mesh.devices.reshape(4, 4, 2, mesh.shape["sr"]), (Y, X, CORE, Z))
    in_specs = (P(None, SR_TM), P(SR_TM, None), P(SR_TM), P(), P(), P(), P())
    out_specs = (P(TM, None), P(SR_TM, None), P())
    return jax.shard_map(local, mesh=split, in_specs=in_specs, out_specs=out_specs, check_vma=False)
```

```python
import jax
import jax.numpy as jnp
from jax import lax
from jax.experimental import pallas as pl
from jax.experimental.pallas import tpu as pltpu
from jax.sharding import Mesh
from jax.sharding import PartitionSpec as P

Y, X, CORE, Z = "tm_0", "tm_1", "tm_2", "sr"
TM = (Y, X, CORE)
SR_TM = (Z, Y, X, CORE)

STEPS = 8
SQUARINGS = 7
LEAPS = 4
FIRST = 4
f32 = jnp.float32
bf16 = jnp.bfloat16
precise = lax.Precision.HIGHEST


def thirds(v):
    a = v.astype(bf16)
    rest = v - a.astype(f32)
    b = rest.astype(bf16)
    c = (rest - b.astype(f32)).astype(bf16)
    return a, b, c


def right(w):
    a, b, c = thirds(w)
    both = jnp.concatenate([a, b], axis=1)
    if w.shape[0] <= 128:
        return both, (jnp.concatenate([c, a], axis=0),)
    return both, (c, a)


def plain(a, b):
    return jnp.dot(a, b, preferred_element_type=f32)


def times(v, w):
    return times_split(thirds(v), w)


def times_split(v, w):
    both, small = w
    n = both.shape[1] // 2
    a, b, c = v
    p, q = plain(a, both), plain(b, both)
    if len(small) == 1:
        least = plain(jnp.concatenate([a, c], axis=1), small[0])
    else:
        least = plain(a, small[0]) + plain(c, small[1])
    return p[:, :n] + (p[:, n:] + q[:, :n] + (q[:, n:] + least))


def high(a, b):
    return times(a, right(b))


def contracted(a, b):
    return lax.dot_general(a, b, (((0,), (0,)), ((), ())), preferred_element_type=f32)


def moved(v, shift, row):
    n = v.shape[0]
    keep = (row >= shift) if shift > 0 else (row < n + shift)
    return jnp.where(keep, pltpu.roll(v, shift % n, 0), 0.0)


def powers(a, n):
    found = [a]
    while len(found) < STEPS:
        more = high(jnp.concatenate(found, axis=0), found[-1])
        found = found + [more[i * n : (i + 1) * n] for i in range(len(found))]
    return found


def kept(blocks_at, count=1):
    both = blocks_at[0]
    small = blocks_at[1]
    if count == 1:
        return both, (jnp.concatenate([small, both[:, : both.shape[1] // 2]], axis=0),)
    return both, (small, both[:, : both.shape[1] // 2])


def beneath(*pieces):
    return tuple(jnp.concatenate(p, axis=0) for p in zip(*pieces))


def pieces_of(w):
    a, b, c = thirds(w)
    return jnp.concatenate([a, b], axis=1), c


def ready_kernel(ft_ref, kt_ref, jt_ref, cov_ref, both_ref, small_ref, drift_ref):
    n = ft_ref.shape[0]
    ft, kt, jt = ft_ref[...], kt_ref[...], jt_ref[...]
    eye = (
        lax.broadcasted_iota(jnp.int32, (n, n), 0) == lax.broadcasted_iota(jnp.int32, (n, n), 1)
    ).astype(f32)

    def put(at, w):
        both, small = pieces_of(w)
        both_ref[at] = both
        small_ref[at] = small

    put(0, kt)
    put(1, eye - high(ft, jt))
    raised = powers(jt, n)
    put(2, ft)
    put(3, high(ft, raised[-1]))
    for k, w in enumerate(raised):
        put(FIRST + k, w)
    power = raised[-1]
    for k in range(FIRST + STEPS, both_ref.shape[0]):
        power = high(power, power)
        put(k, power)
    drift_ref[...] = high(cov_ref[...], jt)


def readied(ft, kt, jt, cov, length):
    n = ft.shape[0]
    count = FIRST + STEPS + (length // STEPS).bit_length() - 2
    vmem = pl.BlockSpec(memory_space=pltpu.VMEM)
    return pl.pallas_call(
        ready_kernel,
        out_shape=(
            jax.ShapeDtypeStruct((count, n, 2 * n), bf16),
            jax.ShapeDtypeStruct((count, n, n), bf16),
            jax.ShapeDtypeStruct((n, n), f32),
        ),
        in_specs=[vmem] * 4,
        out_specs=[vmem] * 3,
        compiler_params=pltpu.CompilerParams(vmem_limit_bytes=16 * 1024 * 1024),
        cost_estimate=pl.CostEstimate(flops=10**9, bytes_accessed=2 * 10**6, transcendentals=0),
        name="ready",
    )(ft, kt, jt, cov)


def begin_kernel(own_ref, kt_ref, ft_ref, power_ref):
    n = ft_ref.shape[0]
    groups = own_ref.shape[0]
    rows = own_ref.shape[1] - n // groups
    info = jnp.concatenate([own_ref[g, rows:] for g in range(groups)], axis=0)
    ft = ft_ref[...]
    a = ft - high(high(ft, info), kt_ref[...])
    found = powers(a, n)
    for _ in range(LEAPS - 1):
        found.append(high(found[-1], found[-1]))
    for k, w in enumerate(found):
        power_ref[k] = w


def begun(own, kt, ft):
    n = ft.shape[0]
    vmem = pl.BlockSpec(memory_space=pltpu.VMEM)
    return pl.pallas_call(
        begin_kernel,
        out_shape=jax.ShapeDtypeStruct((STEPS + LEAPS - 1, n, n), f32),
        in_specs=[vmem] * 3,
        out_specs=vmem,
        compiler_params=pltpu.CompilerParams(vmem_limit_bytes=16 * 1024 * 1024),
        cost_estimate=pl.CostEstimate(flops=10**9, bytes_accessed=2 * 10**6, transcendentals=0),
        name="begin",
    )(own, kt, ft)


def scan_kernel(
    core_ref, place_ref, own_ref, other_ref, both_ref, small_ref, power_ref, cov_ref, drift_ref,
    x_ref, shown_ref, total_ref, previous_ref, lagged_ref, loc_ref, mat_ref,
):
    n = cov_ref.shape[0]
    groups = own_ref.shape[0]
    length = x_ref.shape[0]
    rows = length // (2 * groups)
    blocks = length // STEPS
    first = core_ref[0] == 0
    cov = cov_ref[...]
    held = lambda k: (both_ref[k], small_ref[k])
    pairs = blocks // 2
    row = lax.broadcasted_iota(jnp.int32, (pairs, n), 0)
    levels = blocks.bit_length() - 1
    leap = power_ref[STEPS + LEAPS - 2]
    leaps = [None] * (LEAPS - 1) + [right(leap)]

    def drive(j):
        def half(ref, start):
            parts = [
                ref[g, pl.ds(start, rows // (2 * STEPS), stride=2 * STEPS), :] for g in range(groups)
            ]
            return jnp.concatenate(parts, axis=0)

        found = []
        for start in (j, STEPS + j):
            own, other = half(own_ref, start), half(other_ref, start)
            found += [jnp.where(first, own, other), jnp.where(first, other, own)]
        return jnp.concatenate(found, axis=0)

    step = kept(beneath(pieces_of(power_ref[0]), held(0)), 2)
    state = times(drive(0), kept(held(0)))
    loc_ref[0] = state
    for j in range(1, STEPS):
        state = times(jnp.concatenate([state, drive(j)], axis=1), step)
        loc_ref[j] = state
        if len(leaps) < levels:
            leap = times(leap, leaps[-1])
            leaps.append(right(leap))
    even, odd = state[:pairs], state[pairs:]
    back = kept(beneath(held(FIRST), held(1)), 2)
    both = lambda j: jnp.concatenate([loc_ref[j], power_ref[j]], axis=0)

    def leap_of(level):
        nonlocal leap
        if level < LEAPS - 1:
            return right(power_ref[STEPS - 1 + level])
        if len(leaps) <= level:
            leap = times(leap, leaps[-1])
            leaps.append(right(leap))
        return leaps[level]

    enter = None
    level = 0
    out = times(both(STEPS - 1), kept(held(1)))
    for j in range(STEPS - 1, -1, -1):
        if j < STEPS - 1:
            out = times(jnp.concatenate([out, both(j)], axis=1), back)
        loc_ref[j] = out[:blocks]
        mat_ref[j] = out[blocks:]
        while level < (levels if j == 0 else STEPS - j):
            if level == 0:
                enter = times(even, leap_of(0)) + odd
            else:
                enter = enter + times(moved(enter, 1 << (level - 1), row), leap_of(level))
            level += 1
    entered = moved(enter, 1, row)
    e = jnp.concatenate([entered, times(entered, leap_of(0)) + even], axis=0)
    tail = lax.broadcasted_iota(jnp.int32, (8, n), 0) == 7
    final = jnp.where(tail, enter[pairs - 8 :], 0.0)
    after = times(final, kept(held(2)))
    z = loc_ref[0] + high(e, mat_ref[0])
    even = z[:pairs]
    odd = jnp.concatenate(
        [z[pairs : blocks - 8], z[blocks - 8 :] + times(final, kept(held(3)))], axis=0
    )
    one = kept(held(FIRST + STEPS - 1))
    even = even + times(odd, one)
    for level in range(levels - 1):
        even = even + times(moved(even, -(1 << level), row), kept(held(FIRST + STEPS + level)))
    ahead = moved(even, -1, row)
    odd = odd + times(ahead, one)
    z = jnp.concatenate([even, odd], axis=0)
    coming = jnp.concatenate([odd, ahead[: pairs - 8], ahead[pairs - 8 :] + after], axis=0)
    mixed = thirds(jnp.concatenate([e, coming], axis=1))
    sums = jnp.zeros((n, 2 * n), f32)

    def outer(x, prior):
        xa, xb = x
        pa, pb = prior
        pair = jnp.concatenate([xa, pa], axis=1)
        rest = jnp.concatenate([xb, pb], axis=1)
        return contracted(xa, pair) + (contracted(xb, pair) + contracted(xa, rest))

    opening = prior = thirds(z)[:2]

    def show(j, x):
        x_ref[pl.ds(j, pairs, stride=2 * STEPS), :] = x[:pairs]
        x_ref[pl.ds(STEPS + j, pairs, stride=2 * STEPS), :] = x[pairs:]

    show(0, z)
    for j in range(1, STEPS):
        w = kept(beneath(pieces_of(mat_ref[j]), held(FIRST + STEPS - 1 - j)), 2)
        x = loc_ref[j] + times_split(mixed, w)
        show(j, x)
        here = thirds(x)[:2]
        sums = sums + outer(here, prior)
        prior = here
    prior = jnp.concatenate([moved(x[pairs:], 1, row), x[:pairs]], axis=0)
    sums = sums + outer(opening, thirds(prior)[:2])
    last = jnp.where(tail, x_ref[length - 8 :], 0.0)
    la, lb, _ = thirds(last)
    ends = contracted(la, la) + (contracted(lb, la) + contracted(la, lb))
    total_ref[...] = sums[:, :n] + length * cov
    previous_ref[...] = (sums[:, :n] - ends) + (length - 1) * cov
    lagged_ref[...] = sums[:, n:] + (length - 1) * drift_ref[...]
    count = shown_ref.shape[0]
    shown_ref[...] = x_ref[pl.ds(pl.multiple_of(place_ref[0] * count, count), count), :]


def scanned(core, place, own, other, ready, power, cov, length, parts):
    both, small, drift = ready
    n = cov.shape[0]
    square = jax.ShapeDtypeStruct((n, n), f32)
    vmem = pl.BlockSpec(memory_space=pltpu.VMEM)
    smem = pl.BlockSpec(memory_space=pltpu.SMEM)
    return pl.pallas_call(
        scan_kernel,
        out_shape=(
            jax.ShapeDtypeStruct((length, n), f32),
            jax.ShapeDtypeStruct((length // parts, n), f32),
            square, square, square,
        ),
        in_specs=[smem] * 2 + [vmem] * 7,
        out_specs=[vmem] * 5,
        scratch_shapes=[
            pltpu.VMEM((STEPS, length // STEPS, n), f32),
            pltpu.VMEM((STEPS, n, n), f32),
        ],
        compiler_params=pltpu.CompilerParams(vmem_limit_bytes=44 * 1024 * 1024),
        cost_estimate=pl.CostEstimate(flops=10**10, bytes_accessed=5 * 10**6, transcendentals=0),
        name="scan",
    )(core, place, own, other, both, small, power, cov, drift)


def swept(mats, n):
    row8 = lax.broadcasted_iota(jnp.int32, (8, n), 0)
    lane = lax.broadcasted_iota(jnp.int32, (1, n), 1)
    mats = [[m[8 * g : 8 * g + 8] for g in range(n // 8)] for m in mats]
    for k in range(n):
        found = []
        for m in mats:
            g, o = divmod(k, 8)
            pivot_row = m[g][o : o + 1, :]
            d = 1.0 / pivot_row[:, k : k + 1]
            s = jnp.where(lane == k, d, pivot_row * d)
            new = []
            for i, t in enumerate(m):
                u = jnp.where(lane == k, 0.0, t) - t[:, k : k + 1] * s
                new.append(jnp.where(row8 == o, s, u) if i == g else u)
            found.append(new)
        mats = found
    return [jnp.concatenate(m, axis=0) for m in mats]


def three(v, w):
    a, b, _ = thirds(v)
    c, d, _ = thirds(w)
    n = w.shape[1]
    y = plain(a, jnp.concatenate([c, d], axis=1))
    return y[:, :n] + (y[:, n:] + plain(b, c))


def inverse_kernel(total_ref, previous_ref, lagged_ref, cross_ref, loadings_ref, transition_ref):
    n = total_ref.shape[0]
    eye = (
        lax.broadcasted_iota(jnp.int32, (n, n), 0) == lax.broadcasted_iota(jnp.int32, (n, n), 1)
    ).astype(f32)
    mats = [total_ref[...], previous_ref[...]]
    near, left = [], []
    for m in mats:
        bound = jnp.max(jnp.sum(jnp.abs(m), axis=0, keepdims=True), axis=1, keepdims=True)
        r = eye - m * (1.8 / bound)
        left.append(r)
        near.append((eye + r) * (1.8 / bound))
    for _ in range(SQUARINGS):
        for i in range(2):
            left[i] = three(left[i], left[i])
            near[i] = near[i] + three(near[i], left[i])
    size = jnp.zeros((1, 1), f32)
    for i, (taken_ref, out_ref) in enumerate(
        ((cross_ref, loadings_ref), (lagged_ref, transition_ref))
    ):
        w = right(near[i])
        r = eye - times(mats[i], w)
        first = times(taken_ref[...], w)
        out_ref[...] = first + three(first, r)
        square = jnp.sum(jnp.sum(r * r, axis=0, keepdims=True), axis=1, keepdims=True)
        size = jnp.maximum(size, square)

    @pl.when(jnp.logical_not(size[0, 0] < 1e-6))
    def _():
        one, two = swept([total_ref[...], previous_ref[...]], n)
        loadings_ref[...] = high(cross_ref[...], one)
        transition_ref[...] = high(lagged_ref[...], two)


def inverted(total, previous, lagged, cross):
    vmem = pl.BlockSpec(memory_space=pltpu.VMEM)
    square = jax.ShapeDtypeStruct(total.shape, f32)
    return pl.pallas_call(
        inverse_kernel,
        out_shape=(jax.ShapeDtypeStruct(cross.shape, f32), square),
        in_specs=[vmem] * 4,
        out_specs=[vmem] * 2,
        compiler_params=pltpu.CompilerParams(vmem_limit_bytes=16 * 1024 * 1024),
        cost_estimate=pl.CostEstimate(flops=10**9, bytes_accessed=6 * 10**5, transcendentals=0),
        name="inverse",
    )(total, previous, lagged, cross)


def turned(value, axis, steps):
    count = lax.axis_size(axis)
    return lax.ppermute(value, axis, [(i, (i + steps) % count) for i in range(count)])


def over_z(value):
    count = lax.axis_size(Z)
    value = value + lax.ppermute(value, Z, [(i, i ^ 1) for i in range(count)])
    arrived = [turned(value, Z, 2 * k) for k in range(1, count // 2)]
    return sum(arrived, value)


def local(
    observations, loadings, noise_precision, transition, filter_cov, smoother_gain, smoothed_cov
):
    core = lax.axis_index(CORE)
    position = lax.axis_index(TM)
    length = observations.shape[0]
    width = transition.shape[0]
    half = length // 2
    groups = lax.axis_size((Y, X))
    rows = half // groups
    extra = width // groups
    weighted = noise_precision[:, None] * loadings
    scaled = weighted.astype(bf16)

    info_part = jnp.dot(loadings.T, weighted, precision=precise, preferred_element_type=f32)
    info_part = info_part + turned(info_part, CORE, 1)
    kept_rows, given_rows, factors = lax.optimization_barrier(
        (
            lax.dynamic_slice_in_dim(observations, core * half, half, 0),
            lax.dynamic_slice_in_dim(observations, (1 - core) * half, half, 0),
            scaled,
        )
    )
    given = jnp.dot(given_rows, factors, preferred_element_type=f32)
    mine = jnp.dot(kept_rows, factors, preferred_element_type=f32)
    mine, info_part = lax.optimization_barrier((mine, info_part))
    mine = mine + turned(given, CORE, 1)
    pieces = jnp.concatenate(
        [mine.reshape(groups, rows, width), info_part.reshape(groups, extra, width)], axis=1
    )
    arrived = lax.all_to_all(pieces, (Y, X), split_axis=0, concat_axis=0, tiled=True)
    block = over_z(arrived.sum(axis=0))
    ready = readied(transition.T, filter_cov.T, smoother_gain.T, smoothed_cov, length)
    block, ready = lax.optimization_barrier((block, ready))
    copies = jnp.broadcast_to(block, (groups, *block.shape))
    own = lax.all_to_all(copies, (Y, X), split_axis=0, concat_axis=0, tiled=True)
    other = turned(own, CORE, 1)
    power = begun(own, filter_cov.T, transition.T)
    smoothed, shown, total, previous, lagged = scanned(
        core[None].astype(jnp.int32), position[None].astype(jnp.int32), own, other, ready,
        power, smoothed_cov, length, lax.axis_size(TM),
    )
    cross = jnp.einsum(
        "ts,tk->sk", observations, smoothed.astype(bf16), preferred_element_type=f32
    )
    new_loadings, new_transition = inverted(total, previous, lagged, cross)
    return (shown, new_loadings, new_transition)


def solution(mesh):
    split = Mesh(mesh.devices.reshape(4, 4, 2, mesh.shape["sr"]), (Y, X, CORE, Z))
    in_specs = (P(None, SR_TM), P(SR_TM, None), P(SR_TM), P(), P(), P(), P())
    out_specs = (P(TM, None), P(SR_TM, None), P())
    return jax.shard_map(local, mesh=split, in_specs=in_specs, out_specs=out_specs, check_vma=False)
```

```python
import jax
import jax.numpy as jnp
from jax import lax
from jax.experimental import pallas as pl
from jax.experimental.pallas import tpu as pltpu
from jax.sharding import Mesh
from jax.sharding import PartitionSpec as P

Y, X, CORE, ZH, ZL = "tm_0", "tm_1", "tm_2", "sr_0", "sr_1"
TM = (Y, X, CORE)
SR_TM = (ZH, ZL, Y, X, CORE)
NEAR = (Y, X, ZL)

STEPS = 8
SQUARINGS = 7
LEAPS = 4
FIRST = 4
f32 = jnp.float32
bf16 = jnp.bfloat16
precise = lax.Precision.HIGHEST


def thirds(v):
    a = v.astype(bf16)
    rest = v - a.astype(f32)
    b = rest.astype(bf16)
    c = (rest - b.astype(f32)).astype(bf16)
    return a, b, c


def right(w):
    a, b, c = thirds(w)
    both = jnp.concatenate([a, b], axis=1)
    if w.shape[0] <= 128:
        return both, (jnp.concatenate([c, a], axis=0),)
    return both, (c, a)


def plain(a, b):
    return jnp.dot(a, b, preferred_element_type=f32)


def times(v, w):
    return times_split(thirds(v), w)


def times_split(v, w):
    both, small = w
    n = both.shape[1] // 2
    a, b, c = v
    p, q = plain(a, both), plain(b, both)
    if len(small) == 1:
        least = plain(jnp.concatenate([a, c], axis=1), small[0])
    else:
        least = plain(a, small[0]) + plain(c, small[1])
    return p[:, :n] + (p[:, n:] + q[:, :n] + (q[:, n:] + least))


def high(a, b):
    return times(a, right(b))


def contracted(a, b):
    return lax.dot_general(a, b, (((0,), (0,)), ((), ())), preferred_element_type=f32)


def moved(v, shift, row):
    n = v.shape[0]
    keep = (row >= shift) if shift > 0 else (row < n + shift)
    return jnp.where(keep, pltpu.roll(v, shift % n, 0), 0.0)


def powers(a, n):
    found = [a]
    while len(found) < STEPS:
        more = high(jnp.concatenate(found, axis=0), found[-1])
        found = found + [more[i * n : (i + 1) * n] for i in range(len(found))]
    return found


def kept(blocks_at, count=1):
    both = blocks_at[0]
    small = blocks_at[1]
    if count == 1:
        return both, (jnp.concatenate([small, both[:, : both.shape[1] // 2]], axis=0),)
    return both, (small, both[:, : both.shape[1] // 2])


def beneath(*pieces):
    return tuple(jnp.concatenate(p, axis=0) for p in zip(*pieces))


def pieces_of(w):
    a, b, c = thirds(w)
    return jnp.concatenate([a, b], axis=1), c


def ready_kernel(ft_ref, kt_ref, jt_ref, cov_ref, both_ref, small_ref, drift_ref):
    n = ft_ref.shape[0]
    ft, kt, jt = ft_ref[...], kt_ref[...], jt_ref[...]
    eye = (
        lax.broadcasted_iota(jnp.int32, (n, n), 0) == lax.broadcasted_iota(jnp.int32, (n, n), 1)
    ).astype(f32)

    def put(at, w):
        both, small = pieces_of(w)
        both_ref[at] = both
        small_ref[at] = small

    put(0, kt)
    put(1, eye - high(ft, jt))
    raised = powers(jt, n)
    put(2, ft)
    put(3, high(ft, raised[-1]))
    for k, w in enumerate(raised):
        put(FIRST + k, w)
    power = raised[-1]
    for k in range(FIRST + STEPS, both_ref.shape[0]):
        power = high(power, power)
        put(k, power)
    drift_ref[...] = high(cov_ref[...], jt)


def readied(ft, kt, jt, cov, length):
    n = ft.shape[0]
    count = FIRST + STEPS + (length // STEPS).bit_length() - 2
    vmem = pl.BlockSpec(memory_space=pltpu.VMEM)
    return pl.pallas_call(
        ready_kernel,
        out_shape=(
            jax.ShapeDtypeStruct((count, n, 2 * n), bf16),
            jax.ShapeDtypeStruct((count, n, n), bf16),
            jax.ShapeDtypeStruct((n, n), f32),
        ),
        in_specs=[vmem] * 4,
        out_specs=[vmem] * 3,
        compiler_params=pltpu.CompilerParams(vmem_limit_bytes=16 * 1024 * 1024),
        cost_estimate=pl.CostEstimate(flops=10**9, bytes_accessed=2 * 10**6, transcendentals=0),
        name="ready",
    )(ft, kt, jt, cov)


def begin_kernel(own_ref, kt_ref, ft_ref, power_ref):
    n = ft_ref.shape[0]
    groups = own_ref.shape[0]
    rows = own_ref.shape[1] - 2 * n // groups
    info = jnp.concatenate([own_ref[g, rows:] for g in range(0, groups, 2)], axis=0)
    ft = ft_ref[...]
    a = ft - high(high(ft, info), kt_ref[...])
    found = powers(a, n)
    for _ in range(LEAPS - 1):
        found.append(high(found[-1], found[-1]))
    for k, w in enumerate(found):
        power_ref[k] = w


def begun(own, kt, ft):
    n = ft.shape[0]
    vmem = pl.BlockSpec(memory_space=pltpu.VMEM)
    return pl.pallas_call(
        begin_kernel,
        out_shape=jax.ShapeDtypeStruct((STEPS + LEAPS - 1, n, n), f32),
        in_specs=[vmem] * 3,
        out_specs=vmem,
        compiler_params=pltpu.CompilerParams(vmem_limit_bytes=16 * 1024 * 1024),
        cost_estimate=pl.CostEstimate(flops=10**9, bytes_accessed=2 * 10**6, transcendentals=0),
        name="begin",
    )(own, kt, ft)


def scan_kernel(
    core_ref, place_ref, own_ref, other_ref, both_ref, small_ref, power_ref, cov_ref, drift_ref,
    x_ref, shown_ref, total_ref, previous_ref, lagged_ref, loc_ref, mat_ref,
):
    n = cov_ref.shape[0]
    groups = own_ref.shape[0]
    length = x_ref.shape[0]
    rows = length // (2 * groups)
    blocks = length // STEPS
    first = core_ref[0] == 0
    cov = cov_ref[...]
    held = lambda k: (both_ref[k], small_ref[k])
    pairs = blocks // 2
    row = lax.broadcasted_iota(jnp.int32, (pairs, n), 0)
    levels = blocks.bit_length() - 1
    leap = power_ref[STEPS + LEAPS - 2]
    leaps = [None] * (LEAPS - 1) + [right(leap)]

    def drive(j):
        def half(ref, start):
            parts = [
                ref[g, pl.ds(j, rows // STEPS, stride=STEPS), :] for g in range(start, groups, 2)
            ]
            return jnp.concatenate(parts, axis=0)

        found = []
        for start in range(2):
            own, other = half(own_ref, start), half(other_ref, start)
            found += [jnp.where(first, own, other), jnp.where(first, other, own)]
        return jnp.concatenate(found, axis=0)

    step = kept(beneath(pieces_of(power_ref[0]), held(0)), 2)
    state = times(drive(0), kept(held(0)))
    loc_ref[0] = state
    for j in range(1, STEPS):
        state = times(jnp.concatenate([state, drive(j)], axis=1), step)
        loc_ref[j] = state
        if len(leaps) < levels:
            leap = times(leap, leaps[-1])
            leaps.append(right(leap))
    even, odd = state[:pairs], state[pairs:]
    back = kept(beneath(held(FIRST), held(1)), 2)
    both = lambda j: jnp.concatenate([loc_ref[j], power_ref[j]], axis=0)

    def leap_of(level):
        nonlocal leap
        if level < LEAPS - 1:
            return right(power_ref[STEPS - 1 + level])
        if len(leaps) <= level:
            leap = times(leap, leaps[-1])
            leaps.append(right(leap))
        return leaps[level]

    enter = None
    level = 0
    out = times(both(STEPS - 1), kept(held(1)))
    for j in range(STEPS - 1, -1, -1):
        if j < STEPS - 1:
            out = times(jnp.concatenate([out, both(j)], axis=1), back)
        loc_ref[j] = out[:blocks]
        mat_ref[j] = out[blocks:]
        while level < (levels if j == 0 else STEPS - j):
            if level == 0:
                enter = times(even, leap_of(0)) + odd
            else:
                enter = enter + times(moved(enter, 1 << (level - 1), row), leap_of(level))
            level += 1
    entered = moved(enter, 1, row)
    e = jnp.concatenate([entered, times(entered, leap_of(0)) + even], axis=0)
    tail = lax.broadcasted_iota(jnp.int32, (8, n), 0) == 7
    final = jnp.where(tail, enter[pairs - 8 :], 0.0)
    after = times(final, kept(held(2)))
    z = loc_ref[0] + high(e, mat_ref[0])
    even = z[:pairs]
    odd = jnp.concatenate(
        [z[pairs : blocks - 8], z[blocks - 8 :] + times(final, kept(held(3)))], axis=0
    )
    one = kept(held(FIRST + STEPS - 1))
    even = even + times(odd, one)
    for level in range(levels - 1):
        even = even + times(moved(even, -(1 << level), row), kept(held(FIRST + STEPS + level)))
    ahead = moved(even, -1, row)
    odd = odd + times(ahead, one)
    z = jnp.concatenate([even, odd], axis=0)
    coming = jnp.concatenate([odd, ahead[: pairs - 8], ahead[pairs - 8 :] + after], axis=0)
    mixed = thirds(jnp.concatenate([e, coming], axis=1))
    sums = jnp.zeros((n, 2 * n), f32)

    def outer(x, prior):
        xa, xb = x
        pa, pb = prior
        pair = jnp.concatenate([xa, pa], axis=1)
        rest = jnp.concatenate([xb, pb], axis=1)
        return contracted(xa, pair) + (contracted(xb, pair) + contracted(xa, rest))

    opening = prior = thirds(z)[:2]

    def show(j, x):
        x_ref[pl.ds(j, pairs, stride=2 * STEPS), :] = x[:pairs]
        x_ref[pl.ds(STEPS + j, pairs, stride=2 * STEPS), :] = x[pairs:]

    show(0, z)
    for j in range(1, STEPS):
        w = kept(beneath(pieces_of(mat_ref[j]), held(FIRST + STEPS - 1 - j)), 2)
        x = loc_ref[j] + times_split(mixed, w)
        show(j, x)
        here = thirds(x)[:2]
        sums = sums + outer(here, prior)
        prior = here
    prior = jnp.concatenate([moved(x[pairs:], 1, row), x[:pairs]], axis=0)
    sums = sums + outer(opening, thirds(prior)[:2])
    last = jnp.where(tail, x_ref[length - 8 :], 0.0)
    la, lb, _ = thirds(last)
    ends = contracted(la, la) + (contracted(lb, la) + contracted(la, lb))
    total_ref[...] = sums[:, :n] + length * cov
    previous_ref[...] = (sums[:, :n] - ends) + (length - 1) * cov
    lagged_ref[...] = sums[:, n:] + (length - 1) * drift_ref[...]
    count = shown_ref.shape[0]
    shown_ref[...] = x_ref[pl.ds(pl.multiple_of(place_ref[0] * count, count), count), :]


def scanned(core, place, own, other, ready, power, cov, length, parts):
    both, small, drift = ready
    n = cov.shape[0]
    square = jax.ShapeDtypeStruct((n, n), f32)
    vmem = pl.BlockSpec(memory_space=pltpu.VMEM)
    smem = pl.BlockSpec(memory_space=pltpu.SMEM)
    return pl.pallas_call(
        scan_kernel,
        out_shape=(
            jax.ShapeDtypeStruct((length, n), f32),
            jax.ShapeDtypeStruct((length // parts, n), f32),
            square, square, square,
        ),
        in_specs=[smem] * 2 + [vmem] * 7,
        out_specs=[vmem] * 5,
        scratch_shapes=[
            pltpu.VMEM((STEPS, length // STEPS, n), f32),
            pltpu.VMEM((STEPS, n, n), f32),
        ],
        compiler_params=pltpu.CompilerParams(vmem_limit_bytes=44 * 1024 * 1024),
        cost_estimate=pl.CostEstimate(flops=10**10, bytes_accessed=5 * 10**6, transcendentals=0),
        name="scan",
    )(core, place, own, other, both, small, power, cov, drift)


def swept(mats, n):
    row8 = lax.broadcasted_iota(jnp.int32, (8, n), 0)
    lane = lax.broadcasted_iota(jnp.int32, (1, n), 1)
    mats = [[m[8 * g : 8 * g + 8] for g in range(n // 8)] for m in mats]
    for k in range(n):
        found = []
        for m in mats:
            g, o = divmod(k, 8)
            pivot_row = m[g][o : o + 1, :]
            d = 1.0 / pivot_row[:, k : k + 1]
            s = jnp.where(lane == k, d, pivot_row * d)
            new = []
            for i, t in enumerate(m):
                u = jnp.where(lane == k, 0.0, t) - t[:, k : k + 1] * s
                new.append(jnp.where(row8 == o, s, u) if i == g else u)
            found.append(new)
        mats = found
    return [jnp.concatenate(m, axis=0) for m in mats]


def three(v, w):
    a, b, _ = thirds(v)
    c, d, _ = thirds(w)
    n = w.shape[1]
    y = plain(a, jnp.concatenate([c, d], axis=1))
    return y[:, :n] + (y[:, n:] + plain(b, c))


def inverse_kernel(total_ref, previous_ref, lagged_ref, cross_ref, loadings_ref, transition_ref):
    n = total_ref.shape[0]
    eye = (
        lax.broadcasted_iota(jnp.int32, (n, n), 0) == lax.broadcasted_iota(jnp.int32, (n, n), 1)
    ).astype(f32)
    mats = [total_ref[...], previous_ref[...]]
    near, left = [], []
    for m in mats:
        bound = jnp.max(jnp.sum(jnp.abs(m), axis=0, keepdims=True), axis=1, keepdims=True)
        r = eye - m * (1.8 / bound)
        left.append(r)
        near.append((eye + r) * (1.8 / bound))
    for _ in range(SQUARINGS):
        for i in range(2):
            left[i] = three(left[i], left[i])
            near[i] = near[i] + three(near[i], left[i])
    size = jnp.zeros((1, 1), f32)
    for i, (taken_ref, out_ref) in enumerate(
        ((cross_ref, loadings_ref), (lagged_ref, transition_ref))
    ):
        w = right(near[i])
        r = eye - times(mats[i], w)
        first = times(taken_ref[...], w)
        out_ref[...] = first + three(first, r)
        square = jnp.sum(jnp.sum(r * r, axis=0, keepdims=True), axis=1, keepdims=True)
        size = jnp.maximum(size, square)

    @pl.when(jnp.logical_not(size[0, 0] < 1e-6))
    def _():
        one, two = swept([total_ref[...], previous_ref[...]], n)
        loadings_ref[...] = high(cross_ref[...], one)
        transition_ref[...] = high(lagged_ref[...], two)


def inverted(total, previous, lagged, cross):
    vmem = pl.BlockSpec(memory_space=pltpu.VMEM)
    square = jax.ShapeDtypeStruct(total.shape, f32)
    return pl.pallas_call(
        inverse_kernel,
        out_shape=(jax.ShapeDtypeStruct(cross.shape, f32), square),
        in_specs=[vmem] * 4,
        out_specs=[vmem] * 2,
        compiler_params=pltpu.CompilerParams(vmem_limit_bytes=16 * 1024 * 1024),
        cost_estimate=pl.CostEstimate(flops=10**9, bytes_accessed=6 * 10**5, transcendentals=0),
        name="inverse",
    )(total, previous, lagged, cross)


def turned(value, axis, steps):
    count = lax.axis_size(axis)
    return lax.ppermute(value, axis, [(i, (i + steps) % count) for i in range(count)])


def over_far(value):
    return sum([turned(value, ZH, k) for k in range(1, lax.axis_size(ZH))], value)


def local(
    observations, loadings, noise_precision, transition, filter_cov, smoother_gain, smoothed_cov
):
    core = lax.axis_index(CORE)
    position = lax.axis_index(TM)
    length = observations.shape[0]
    width = transition.shape[0]
    half = length // 2
    groups = lax.axis_size(NEAR)
    rows = half // groups
    extra = 2 * width // groups
    weighted = noise_precision[:, None] * loadings
    scaled = weighted.astype(bf16)

    info_part = jnp.dot(loadings.T, weighted, precision=precise, preferred_element_type=f32)
    info_part = info_part + turned(info_part, CORE, 1)
    kept_rows, given_rows, factors = lax.optimization_barrier(
        (
            lax.dynamic_slice_in_dim(observations, core * half, half, 0),
            lax.dynamic_slice_in_dim(observations, (1 - core) * half, half, 0),
            scaled,
        )
    )
    given = jnp.dot(given_rows, factors, preferred_element_type=f32)
    mine = jnp.dot(kept_rows, factors, preferred_element_type=f32)
    mine, info_part = lax.optimization_barrier((mine, info_part))
    mine = mine + turned(given, CORE, 1)
    mine = mine.reshape(groups // 2, rows // STEPS, 2, STEPS, width).transpose(0, 2, 1, 3, 4)
    info_part = info_part.reshape(groups // 2, 1, extra, width)
    pieces = jnp.concatenate(
        [
            mine.reshape(groups, rows, width),
            jnp.pad(info_part, ((0, 0), (0, 1), (0, 0), (0, 0))).reshape(groups, extra, width),
        ],
        axis=1,
    )
    arrived = lax.all_to_all(pieces, NEAR, split_axis=0, concat_axis=0, tiled=True)
    block = over_far(arrived.sum(axis=0))
    ready = readied(transition.T, filter_cov.T, smoother_gain.T, smoothed_cov, length)
    block, ready = lax.optimization_barrier((block, ready))
    copies = jnp.broadcast_to(block, (groups, *block.shape))
    own = lax.all_to_all(copies, NEAR, split_axis=0, concat_axis=0, tiled=True)
    other = turned(own, CORE, 1)
    power = begun(own, filter_cov.T, transition.T)
    smoothed, shown, total, previous, lagged = scanned(
        core[None].astype(jnp.int32), position[None].astype(jnp.int32), own, other, ready,
        power, smoothed_cov, length, lax.axis_size(TM),
    )
    cross = jnp.einsum(
        "ts,tk->sk", observations, smoothed.astype(bf16), preferred_element_type=f32
    )
    new_loadings, new_transition = inverted(total, previous, lagged, cross)
    return (shown, new_loadings, new_transition)


def solution(mesh):
    near = mesh.devices.reshape(4, 4, 2, mesh.shape["sr"] // 2, 2)
    split = Mesh(near, (Y, X, CORE, ZH, ZL))
    in_specs = (P(None, SR_TM), P(SR_TM, None), P(SR_TM), P(), P(), P(), P())
    out_specs = (P(TM, None), P(SR_TM, None), P())
    return jax.shard_map(local, mesh=split, in_specs=in_specs, out_specs=out_specs, check_vma=False)
```

```python
import jax
import jax.numpy as jnp
from jax import lax
from jax.experimental.layout import Layout, with_layout_constraint
from jax.experimental import pallas as pl
from jax.experimental.pallas import tpu as pltpu
from jax.sharding import Mesh
from jax.sharding import PartitionSpec as P

Y, X, CORE, ZH, ZL = "tm_0", "tm_1", "tm_2", "sr_0", "sr_1"
TM = (Y, X, CORE)
SR_TM = (ZH, ZL, Y, X, CORE)
NEAR = (Y, X, ZL)

STEPS = 8
SQUARINGS = 7
LEAPS = 4
FIRST = 4
f32 = jnp.float32
bf16 = jnp.bfloat16
precise = lax.Precision.HIGHEST


def thirds(v):
    a = v.astype(bf16)
    rest = v - a.astype(f32)
    b = rest.astype(bf16)
    c = (rest - b.astype(f32)).astype(bf16)
    return a, b, c


def right(w):
    a, b, c = thirds(w)
    both = jnp.concatenate([a, b], axis=1)
    if w.shape[0] <= 128:
        return both, (jnp.concatenate([c, a], axis=0),)
    return both, (c, a)


def plain(a, b):
    return jnp.dot(a, b, preferred_element_type=f32)


def times(v, w):
    return times_split(thirds(v), w)


def times_split(v, w):
    both, small = w
    n = both.shape[1] // 2
    a, b, c = v
    p, q = plain(a, both), plain(b, both)
    if len(small) == 1:
        least = plain(jnp.concatenate([a, c], axis=1), small[0])
    else:
        least = plain(a, small[0]) + plain(c, small[1])
    return p[:, :n] + (p[:, n:] + q[:, :n] + (q[:, n:] + least))


def high(a, b):
    return times(a, right(b))


def contracted(a, b):
    return lax.dot_general(a, b, (((0,), (0,)), ((), ())), preferred_element_type=f32)


def moved(v, shift, row):
    n = v.shape[0]
    keep = (row >= shift) if shift > 0 else (row < n + shift)
    return jnp.where(keep, pltpu.roll(v, shift % n, 0), 0.0)


def powers(a, n):
    found = [a]
    while len(found) < STEPS:
        more = high(jnp.concatenate(found, axis=0), found[-1])
        found = found + [more[i * n : (i + 1) * n] for i in range(len(found))]
    return found


def kept(blocks_at, count=1):
    both = blocks_at[0]
    small = blocks_at[1]
    if count == 1:
        return both, (jnp.concatenate([small, both[:, : both.shape[1] // 2]], axis=0),)
    return both, (small, both[:, : both.shape[1] // 2])


def beneath(*pieces):
    return tuple(jnp.concatenate(p, axis=0) for p in zip(*pieces))


def pieces_of(w):
    a, b, c = thirds(w)
    return jnp.concatenate([a, b], axis=1), c


def ready_kernel(ft_ref, kt_ref, jt_ref, cov_ref, both_ref, small_ref, drift_ref):
    n = ft_ref.shape[0]
    ft, kt, jt = ft_ref[...], kt_ref[...], jt_ref[...]
    eye = (
        lax.broadcasted_iota(jnp.int32, (n, n), 0) == lax.broadcasted_iota(jnp.int32, (n, n), 1)
    ).astype(f32)

    def put(at, w):
        both, small = pieces_of(w)
        both_ref[at] = both
        small_ref[at] = small

    put(0, kt)
    put(1, eye - high(ft, jt))
    raised = powers(jt, n)
    put(2, ft)
    put(3, high(ft, raised[-1]))
    for k, w in enumerate(raised):
        put(FIRST + k, w)
    power = raised[-1]
    for k in range(FIRST + STEPS, both_ref.shape[0]):
        power = high(power, power)
        put(k, power)
    drift_ref[...] = high(cov_ref[...], jt)


def readied(ft, kt, jt, cov, length):
    n = ft.shape[0]
    count = FIRST + STEPS + (length // STEPS).bit_length() - 2
    vmem = pl.BlockSpec(memory_space=pltpu.VMEM)
    return pl.pallas_call(
        ready_kernel,
        out_shape=(
            jax.ShapeDtypeStruct((count, n, 2 * n), bf16),
            jax.ShapeDtypeStruct((count, n, n), bf16),
            jax.ShapeDtypeStruct((n, n), f32),
        ),
        in_specs=[vmem] * 4,
        out_specs=[vmem] * 3,
        compiler_params=pltpu.CompilerParams(vmem_limit_bytes=16 * 1024 * 1024),
        cost_estimate=pl.CostEstimate(flops=10**9, bytes_accessed=2 * 10**6, transcendentals=0),
        name="ready",
    )(ft, kt, jt, cov)


def begin_kernel(own_ref, kt_ref, ft_ref, power_ref):
    n = ft_ref.shape[0]
    groups = own_ref.shape[0]
    rows = own_ref.shape[1] - 2 * n // groups
    info = jnp.concatenate([own_ref[g, rows:] for g in range(0, groups, 2)], axis=0)
    ft = ft_ref[...]
    a = ft - high(high(ft, info), kt_ref[...])
    found = powers(a, n)
    for _ in range(LEAPS - 1):
        found.append(high(found[-1], found[-1]))
    for k, w in enumerate(found):
        power_ref[k] = w


def begun(own, kt, ft):
    n = ft.shape[0]
    vmem = pl.BlockSpec(memory_space=pltpu.VMEM)
    return pl.pallas_call(
        begin_kernel,
        out_shape=jax.ShapeDtypeStruct((STEPS + LEAPS - 1, n, n), f32),
        in_specs=[vmem] * 3,
        out_specs=vmem,
        compiler_params=pltpu.CompilerParams(vmem_limit_bytes=16 * 1024 * 1024),
        cost_estimate=pl.CostEstimate(flops=10**9, bytes_accessed=2 * 10**6, transcendentals=0),
        name="begin",
    )(own, kt, ft)


def scan_kernel(
    core_ref, place_ref, own_ref, other_ref, both_ref, small_ref, power_ref, cov_ref, drift_ref,
    x_ref, shown_ref, total_ref, previous_ref, lagged_ref, loc_ref, mat_ref,
):
    n = cov_ref.shape[0]
    groups = own_ref.shape[0]
    length = x_ref.shape[0]
    rows = length // (2 * groups)
    blocks = length // STEPS
    first = core_ref[0] == 0
    cov = cov_ref[...]
    held = lambda k: (both_ref[k], small_ref[k])
    pairs = blocks // 2
    row = lax.broadcasted_iota(jnp.int32, (pairs, n), 0)
    levels = blocks.bit_length() - 1
    leap = power_ref[STEPS + LEAPS - 2]
    leaps = [None] * (LEAPS - 1) + [right(leap)]

    def drive(j):
        def half(ref, start):
            parts = [
                ref[g, pl.ds(j, rows // STEPS, stride=STEPS), :] for g in range(start, groups, 2)
            ]
            return jnp.concatenate(parts, axis=0)

        found = []
        for start in range(2):
            own, other = half(own_ref, start), half(other_ref, start)
            found += [jnp.where(first, own, other), jnp.where(first, other, own)]
        return jnp.concatenate(found, axis=0)

    step = kept(beneath(pieces_of(power_ref[0]), held(0)), 2)
    state = times(drive(0), kept(held(0)))
    loc_ref[0] = state
    for j in range(1, STEPS):
        state = times(jnp.concatenate([state, drive(j)], axis=1), step)
        loc_ref[j] = state
        if len(leaps) < levels:
            leap = times(leap, leaps[-1])
            leaps.append(right(leap))
    even, odd = state[:pairs], state[pairs:]
    back = kept(beneath(held(FIRST), held(1)), 2)
    both = lambda j: jnp.concatenate([loc_ref[j], power_ref[j]], axis=0)

    def leap_of(level):
        nonlocal leap
        if level < LEAPS - 1:
            return right(power_ref[STEPS - 1 + level])
        if len(leaps) <= level:
            leap = times(leap, leaps[-1])
            leaps.append(right(leap))
        return leaps[level]

    enter = None
    level = 0
    out = times(both(STEPS - 1), kept(held(1)))
    for j in range(STEPS - 1, -1, -1):
        if j < STEPS - 1:
            out = times(jnp.concatenate([out, both(j)], axis=1), back)
        loc_ref[j] = out[:blocks]
        mat_ref[j] = out[blocks:]
        while level < (levels if j == 0 else STEPS - j):
            if level == 0:
                enter = times(even, leap_of(0)) + odd
            else:
                enter = enter + times(moved(enter, 1 << (level - 1), row), leap_of(level))
            level += 1
    entered = moved(enter, 1, row)
    e = jnp.concatenate([entered, times(entered, leap_of(0)) + even], axis=0)
    tail = lax.broadcasted_iota(jnp.int32, (8, n), 0) == 7
    final = jnp.where(tail, enter[pairs - 8 :], 0.0)
    after = times(final, kept(held(2)))
    z = loc_ref[0] + high(e, mat_ref[0])
    even = z[:pairs]
    odd = jnp.concatenate(
        [z[pairs : blocks - 8], z[blocks - 8 :] + times(final, kept(held(3)))], axis=0
    )
    one = kept(held(FIRST + STEPS - 1))
    even = even + times(odd, one)
    for level in range(levels - 1):
        even = even + times(moved(even, -(1 << level), row), kept(held(FIRST + STEPS + level)))
    ahead = moved(even, -1, row)
    odd = odd + times(ahead, one)
    z = jnp.concatenate([even, odd], axis=0)
    coming = jnp.concatenate([odd, ahead[: pairs - 8], ahead[pairs - 8 :] + after], axis=0)
    mixed = thirds(jnp.concatenate([e, coming], axis=1))
    sums = jnp.zeros((n, 2 * n), f32)

    def outer(x, prior):
        xa, xb = x
        pa, pb = prior
        pair = jnp.concatenate([xa, pa], axis=1)
        rest = jnp.concatenate([xb, pb], axis=1)
        return contracted(xa, pair) + (contracted(xb, pair) + contracted(xa, rest))

    opening = prior = thirds(z)[:2]

    def show(j, x):
        x_ref[pl.ds(j, pairs, stride=2 * STEPS), :] = x[:pairs]
        x_ref[pl.ds(STEPS + j, pairs, stride=2 * STEPS), :] = x[pairs:]

    show(0, z)
    for j in range(1, STEPS):
        w = kept(beneath(pieces_of(mat_ref[j]), held(FIRST + STEPS - 1 - j)), 2)
        x = loc_ref[j] + times_split(mixed, w)
        show(j, x)
        here = thirds(x)[:2]
        sums = sums + outer(here, prior)
        prior = here
    prior = jnp.concatenate([moved(x[pairs:], 1, row), x[:pairs]], axis=0)
    sums = sums + outer(opening, thirds(prior)[:2])
    last = jnp.where(tail, x_ref[length - 8 :], 0.0)
    la, lb, _ = thirds(last)
    ends = contracted(la, la) + (contracted(lb, la) + contracted(la, lb))
    total_ref[...] = sums[:, :n] + length * cov
    previous_ref[...] = (sums[:, :n] - ends) + (length - 1) * cov
    lagged_ref[...] = sums[:, n:] + (length - 1) * drift_ref[...]
    count = shown_ref.shape[0]
    shown_ref[...] = x_ref[pl.ds(pl.multiple_of(place_ref[0] * count, count), count), :]


def scanned(core, place, own, other, ready, power, cov, length, parts):
    both, small, drift = ready
    n = cov.shape[0]
    square = jax.ShapeDtypeStruct((n, n), f32)
    vmem = pl.BlockSpec(memory_space=pltpu.VMEM)
    smem = pl.BlockSpec(memory_space=pltpu.SMEM)
    return pl.pallas_call(
        scan_kernel,
        out_shape=(
            jax.ShapeDtypeStruct((length, n), f32),
            jax.ShapeDtypeStruct((length // parts, n), f32),
            square, square, square,
        ),
        in_specs=[smem] * 2 + [vmem] * 7,
        out_specs=[vmem] * 5,
        scratch_shapes=[
            pltpu.VMEM((STEPS, length // STEPS, n), f32),
            pltpu.VMEM((STEPS, n, n), f32),
        ],
        compiler_params=pltpu.CompilerParams(vmem_limit_bytes=44 * 1024 * 1024),
        cost_estimate=pl.CostEstimate(flops=10**10, bytes_accessed=5 * 10**6, transcendentals=0),
        name="scan",
    )(core, place, own, other, both, small, power, cov, drift)


def swept(mats, n):
    row8 = lax.broadcasted_iota(jnp.int32, (8, n), 0)
    lane = lax.broadcasted_iota(jnp.int32, (1, n), 1)
    mats = [[m[8 * g : 8 * g + 8] for g in range(n // 8)] for m in mats]
    for k in range(n):
        found = []
        for m in mats:
            g, o = divmod(k, 8)
            pivot_row = m[g][o : o + 1, :]
            d = 1.0 / pivot_row[:, k : k + 1]
            s = jnp.where(lane == k, d, pivot_row * d)
            new = []
            for i, t in enumerate(m):
                u = jnp.where(lane == k, 0.0, t) - t[:, k : k + 1] * s
                new.append(jnp.where(row8 == o, s, u) if i == g else u)
            found.append(new)
        mats = found
    return [jnp.concatenate(m, axis=0) for m in mats]


def three(v, w):
    a, b, _ = thirds(v)
    c, d, _ = thirds(w)
    n = w.shape[1]
    y = plain(a, jnp.concatenate([c, d], axis=1))
    return y[:, :n] + (y[:, n:] + plain(b, c))


def inverse_kernel(total_ref, previous_ref, lagged_ref, cross_ref, loadings_ref, transition_ref):
    n = total_ref.shape[0]
    eye = (
        lax.broadcasted_iota(jnp.int32, (n, n), 0) == lax.broadcasted_iota(jnp.int32, (n, n), 1)
    ).astype(f32)
    mats = [total_ref[...], previous_ref[...]]
    near, left = [], []
    for m in mats:
        bound = jnp.max(jnp.sum(jnp.abs(m), axis=0, keepdims=True), axis=1, keepdims=True)
        r = eye - m * (1.8 / bound)
        left.append(r)
        near.append((eye + r) * (1.8 / bound))
    for _ in range(SQUARINGS):
        for i in range(2):
            left[i] = three(left[i], left[i])
            near[i] = near[i] + three(near[i], left[i])
    size = jnp.zeros((1, 1), f32)
    for i, (taken_ref, out_ref) in enumerate(
        ((cross_ref, loadings_ref), (lagged_ref, transition_ref))
    ):
        w = right(near[i])
        r = eye - times(mats[i], w)
        first = times(taken_ref[...], w)
        out_ref[...] = first + three(first, r)
        square = jnp.sum(jnp.sum(r * r, axis=0, keepdims=True), axis=1, keepdims=True)
        size = jnp.maximum(size, square)

    @pl.when(jnp.logical_not(size[0, 0] < 1e-6))
    def _():
        one, two = swept([total_ref[...], previous_ref[...]], n)
        loadings_ref[...] = high(cross_ref[...], one)
        transition_ref[...] = high(lagged_ref[...], two)


def inverted(total, previous, lagged, cross):
    vmem = pl.BlockSpec(memory_space=pltpu.VMEM)
    square = jax.ShapeDtypeStruct(total.shape, f32)
    return pl.pallas_call(
        inverse_kernel,
        out_shape=(jax.ShapeDtypeStruct(cross.shape, f32), square),
        in_specs=[vmem] * 4,
        out_specs=[vmem] * 2,
        compiler_params=pltpu.CompilerParams(vmem_limit_bytes=16 * 1024 * 1024),
        cost_estimate=pl.CostEstimate(flops=10**9, bytes_accessed=6 * 10**5, transcendentals=0),
        name="inverse",
    )(total, previous, lagged, cross)


def turned(value, axis, steps):
    count = lax.axis_size(axis)
    return lax.ppermute(value, axis, [(i, (i + steps) % count) for i in range(count)])


def over_far(value):
    return sum([turned(value, ZH, k) for k in range(1, lax.axis_size(ZH))], value)


def local(
    observations, loadings, noise_precision, transition, filter_cov, smoother_gain, smoothed_cov
):
    core = lax.axis_index(CORE)
    position = lax.axis_index(TM)
    length = observations.shape[0]
    width = transition.shape[0]
    half = length // 2
    groups = lax.axis_size(NEAR)
    rows = half // groups
    extra = 2 * width // groups
    weighted = noise_precision[:, None] * loadings
    scaled = weighted.astype(bf16)

    info_part = jnp.dot(loadings.T, weighted, precision=precise, preferred_element_type=f32)
    info_part = info_part + turned(info_part, CORE, 1)
    window, factors = lax.optimization_barrier((observations, scaled))
    whole = jnp.dot(window, factors, preferred_element_type=f32)
    whole = with_layout_constraint(whole, Layout(major_to_minor=(0, 1)))
    given = lax.dynamic_slice_in_dim(whole, (1 - core) * half, half, 0)
    mine = lax.dynamic_slice_in_dim(whole, core * half, half, 0)
    given, mine = lax.optimization_barrier((given, mine))
    mine = mine + turned(given, CORE, 1)
    mine = mine.reshape(groups // 2, rows // STEPS, 2, STEPS, width).transpose(0, 2, 1, 3, 4)
    info_part = info_part.reshape(groups // 2, 1, extra, width)
    pieces = jnp.concatenate(
        [
            mine.reshape(groups, rows, width),
            jnp.pad(info_part, ((0, 0), (0, 1), (0, 0), (0, 0))).reshape(groups, extra, width),
        ],
        axis=1,
    )
    arrived = lax.all_to_all(pieces, NEAR, split_axis=0, concat_axis=0, tiled=True)
    arrived, transition, filter_cov, smoother_gain, smoothed_cov = lax.optimization_barrier(
        (arrived, transition, filter_cov, smoother_gain, smoothed_cov)
    )
    block = over_far(arrived.sum(axis=0))
    ready = readied(transition.T, filter_cov.T, smoother_gain.T, smoothed_cov, length)
    block, ready = lax.optimization_barrier((block, ready))
    copies = jnp.broadcast_to(block, (groups, *block.shape))
    own = lax.all_to_all(copies, NEAR, split_axis=0, concat_axis=0, tiled=True)
    other = turned(own, CORE, 1)
    power = begun(own, filter_cov.T, transition.T)
    smoothed, shown, total, previous, lagged = scanned(
        core[None].astype(jnp.int32), position[None].astype(jnp.int32), own, other, ready,
        power, smoothed_cov, length, lax.axis_size(TM),
    )
    cross = jnp.einsum(
        "ts,tk->sk", observations, smoothed.astype(bf16), preferred_element_type=f32
    )
    new_loadings, new_transition = inverted(total, previous, lagged, cross)
    return (shown, new_loadings, new_transition)


def solution(mesh):
    near = mesh.devices.reshape(4, 4, 2, mesh.shape["sr"] // 2, 2)
    split = Mesh(near, (Y, X, CORE, ZH, ZL))
    in_specs = (P(None, SR_TM), P(SR_TM, None), P(SR_TM), P(), P(), P(), P())
    out_specs = (P(TM, None), P(SR_TM, None), P())
    return jax.shard_map(local, mesh=split, in_specs=in_specs, out_specs=out_specs, check_vma=False)
```

```python
import jax
import jax.numpy as jnp
from jax import lax
from jax.experimental import pallas as pl
from jax.experimental.pallas import tpu as pltpu
from jax.sharding import Mesh
from jax.sharding import PartitionSpec as P

Y, X, CORE, Z = "tm_0", "tm_1", "tm_2", "sr"
TM = (Y, X, CORE)
SR_TM = (Z, Y, X, CORE)

STEPS = 8
SQUARINGS = 7
LEAPS = 4
FIRST = 4
f32 = jnp.float32
bf16 = jnp.bfloat16
precise = lax.Precision.HIGHEST


def thirds(v):
    a = v.astype(bf16)
    rest = v - a.astype(f32)
    b = rest.astype(bf16)
    c = (rest - b.astype(f32)).astype(bf16)
    return a, b, c


def right(w):
    a, b, c = thirds(w)
    both = jnp.concatenate([a, b], axis=1)
    if w.shape[0] <= 128:
        return both, (jnp.concatenate([c, a], axis=0),)
    return both, (c, a)


def plain(a, b):
    return jnp.dot(a, b, preferred_element_type=f32)


def times(v, w):
    return times_split(thirds(v), w)


def times_split(v, w):
    both, small = w
    n = both.shape[1] // 2
    a, b, c = v
    p, q = plain(a, both), plain(b, both)
    if len(small) == 1:
        least = plain(jnp.concatenate([a, c], axis=1), small[0])
    else:
        least = plain(a, small[0]) + plain(c, small[1])
    return p[:, :n] + (p[:, n:] + q[:, :n] + (q[:, n:] + least))


def high(a, b):
    return times(a, right(b))


def contracted(a, b):
    return lax.dot_general(a, b, (((0,), (0,)), ((), ())), preferred_element_type=f32)


def moved(v, shift, row):
    n = v.shape[0]
    keep = (row >= shift) if shift > 0 else (row < n + shift)
    return jnp.where(keep, pltpu.roll(v, shift % n, 0), 0.0)


def powers(a, n):
    found = [a]
    while len(found) < STEPS:
        more = high(jnp.concatenate(found, axis=0), found[-1])
        found = found + [more[i * n : (i + 1) * n] for i in range(len(found))]
    return found


def kept(blocks_at, count=1):
    both = blocks_at[0]
    small = blocks_at[1]
    if count == 1:
        return both, (jnp.concatenate([small, both[:, : both.shape[1] // 2]], axis=0),)
    return both, (small, both[:, : both.shape[1] // 2])


def beneath(*pieces):
    return tuple(jnp.concatenate(p, axis=0) for p in zip(*pieces))


def pieces_of(w):
    a, b, c = thirds(w)
    return jnp.concatenate([a, b], axis=1), c


def ready_kernel(ft_ref, kt_ref, jt_ref, cov_ref, both_ref, small_ref, drift_ref):
    n = ft_ref.shape[0]
    ft, kt, jt = ft_ref[...], kt_ref[...], jt_ref[...]
    eye = (
        lax.broadcasted_iota(jnp.int32, (n, n), 0) == lax.broadcasted_iota(jnp.int32, (n, n), 1)
    ).astype(f32)

    def put(at, w):
        both, small = pieces_of(w)
        both_ref[at] = both
        small_ref[at] = small

    put(0, kt)
    put(1, eye - high(ft, jt))
    raised = powers(jt, n)
    put(2, ft)
    put(3, high(ft, raised[-1]))
    for k, w in enumerate(raised):
        put(FIRST + k, w)
    power = raised[-1]
    for k in range(FIRST + STEPS, both_ref.shape[0]):
        power = high(power, power)
        put(k, power)
    drift_ref[...] = high(cov_ref[...], jt)


def readied(ft, kt, jt, cov, length):
    n = ft.shape[0]
    count = FIRST + STEPS + (length // STEPS).bit_length() - 2
    vmem = pl.BlockSpec(memory_space=pltpu.VMEM)
    return pl.pallas_call(
        ready_kernel,
        out_shape=(
            jax.ShapeDtypeStruct((count, n, 2 * n), bf16),
            jax.ShapeDtypeStruct((count, n, n), bf16),
            jax.ShapeDtypeStruct((n, n), f32),
        ),
        in_specs=[vmem] * 4,
        out_specs=[vmem] * 3,
        compiler_params=pltpu.CompilerParams(vmem_limit_bytes=16 * 1024 * 1024),
        cost_estimate=pl.CostEstimate(flops=10**9, bytes_accessed=2 * 10**6, transcendentals=0),
        name="ready",
    )(ft, kt, jt, cov)


def begin_kernel(own_ref, kt_ref, ft_ref, power_ref):
    n = ft_ref.shape[0]
    groups = own_ref.shape[0]
    rows = own_ref.shape[1] - n // groups
    info = jnp.concatenate([own_ref[g, rows:] for g in range(groups)], axis=0)
    ft = ft_ref[...]
    a = ft - high(high(ft, info), kt_ref[...])
    found = powers(a, n)
    for _ in range(LEAPS - 1):
        found.append(high(found[-1], found[-1]))
    for k, w in enumerate(found):
        power_ref[k] = w


def begun(own, kt, ft):
    n = ft.shape[0]
    vmem = pl.BlockSpec(memory_space=pltpu.VMEM)
    return pl.pallas_call(
        begin_kernel,
        out_shape=jax.ShapeDtypeStruct((STEPS + LEAPS - 1, n, n), f32),
        in_specs=[vmem] * 3,
        out_specs=vmem,
        compiler_params=pltpu.CompilerParams(vmem_limit_bytes=16 * 1024 * 1024),
        cost_estimate=pl.CostEstimate(flops=10**9, bytes_accessed=2 * 10**6, transcendentals=0),
        name="begin",
    )(own, kt, ft)


def scan_kernel(
    core_ref, place_ref, own_ref, other_ref, both_ref, small_ref, power_ref, cov_ref, drift_ref,
    x_ref, shown_ref, total_ref, previous_ref, lagged_ref, loc_ref, mat_ref,
):
    n = cov_ref.shape[0]
    groups = own_ref.shape[0]
    length = x_ref.shape[0]
    rows = length // (2 * groups)
    blocks = length // STEPS
    first = core_ref[0] == 0
    cov = cov_ref[...]
    held = lambda k: (both_ref[k], small_ref[k])
    pairs = blocks // 2
    row = lax.broadcasted_iota(jnp.int32, (pairs, n), 0)
    levels = blocks.bit_length() - 1
    leap = power_ref[STEPS + LEAPS - 2]
    leaps = [None] * (LEAPS - 1) + [right(leap)]

    def drive(j):
        def half(ref, start):
            parts = [
                ref[g, pl.ds(start, rows // (2 * STEPS), stride=2 * STEPS), :] for g in range(groups)
            ]
            return jnp.concatenate(parts, axis=0)

        found = []
        for start in (j, STEPS + j):
            own, other = half(own_ref, start), half(other_ref, start)
            found += [jnp.where(first, own, other), jnp.where(first, other, own)]
        return jnp.concatenate(found, axis=0)

    step = kept(beneath(pieces_of(power_ref[0]), held(0)), 2)
    state = times(drive(0), kept(held(0)))
    loc_ref[0] = state
    for j in range(1, STEPS):
        state = times(jnp.concatenate([state, drive(j)], axis=1), step)
        loc_ref[j] = state
        if len(leaps) < levels:
            leap = times(leap, leaps[-1])
            leaps.append(right(leap))
    even, odd = state[:pairs], state[pairs:]
    back = kept(beneath(held(FIRST), held(1)), 2)
    both = lambda j: jnp.concatenate([loc_ref[j], power_ref[j]], axis=0)

    def leap_of(level):
        nonlocal leap
        if level < LEAPS - 1:
            return right(power_ref[STEPS - 1 + level])
        if len(leaps) <= level:
            leap = times(leap, leaps[-1])
            leaps.append(right(leap))
        return leaps[level]

    enter = None
    level = 0
    out = times(both(STEPS - 1), kept(held(1)))
    for j in range(STEPS - 1, -1, -1):
        if j < STEPS - 1:
            out = times(jnp.concatenate([out, both(j)], axis=1), back)
        loc_ref[j] = out[:blocks]
        mat_ref[j] = out[blocks:]
        while level < (levels if j == 0 else STEPS - j):
            if level == 0:
                enter = times(even, leap_of(0)) + odd
            else:
                enter = enter + times(moved(enter, 1 << (level - 1), row), leap_of(level))
            level += 1
    entered = moved(enter, 1, row)
    e = jnp.concatenate([entered, times(entered, leap_of(0)) + even], axis=0)
    tail = lax.broadcasted_iota(jnp.int32, (8, n), 0) == 7
    final = jnp.where(tail, enter[pairs - 8 :], 0.0)
    after = times(final, kept(held(2)))
    z = loc_ref[0] + high(e, mat_ref[0])
    even = z[:pairs]
    odd = jnp.concatenate(
        [z[pairs : blocks - 8], z[blocks - 8 :] + times(final, kept(held(3)))], axis=0
    )
    one = kept(held(FIRST + STEPS - 1))
    even = even + times(odd, one)
    for level in range(levels - 1):
        even = even + times(moved(even, -(1 << level), row), kept(held(FIRST + STEPS + level)))
    ahead = moved(even, -1, row)
    odd = odd + times(ahead, one)
    z = jnp.concatenate([even, odd], axis=0)
    coming = jnp.concatenate([odd, ahead[: pairs - 8], ahead[pairs - 8 :] + after], axis=0)
    mixed = thirds(jnp.concatenate([e, coming], axis=1))
    sums = jnp.zeros((n, 2 * n), f32)

    def outer(x, prior):
        xa, xb = x
        pa, pb = prior
        pair = jnp.concatenate([xa, pa], axis=1)
        rest = jnp.concatenate([xb, pb], axis=1)
        return contracted(xa, pair) + (contracted(xb, pair) + contracted(xa, rest))

    opening = prior = thirds(z)[:2]

    def show(j, x):
        x_ref[pl.ds(j, pairs, stride=2 * STEPS), :] = x[:pairs]
        x_ref[pl.ds(STEPS + j, pairs, stride=2 * STEPS), :] = x[pairs:]

    show(0, z)
    for j in range(1, STEPS):
        w = kept(beneath(pieces_of(mat_ref[j]), held(FIRST + STEPS - 1 - j)), 2)
        x = loc_ref[j] + times_split(mixed, w)
        show(j, x)
        here = thirds(x)[:2]
        sums = sums + outer(here, prior)
        prior = here
    prior = jnp.concatenate([moved(x[pairs:], 1, row), x[:pairs]], axis=0)
    sums = sums + outer(opening, thirds(prior)[:2])
    last = jnp.where(tail, x_ref[length - 8 :], 0.0)
    la, lb, _ = thirds(last)
    ends = contracted(la, la) + (contracted(lb, la) + contracted(la, lb))
    total_ref[...] = sums[:, :n] + length * cov
    previous_ref[...] = (sums[:, :n] - ends) + (length - 1) * cov
    lagged_ref[...] = sums[:, n:] + (length - 1) * drift_ref[...]
    count = shown_ref.shape[0]
    shown_ref[...] = x_ref[pl.ds(pl.multiple_of(place_ref[0] * count, count), count), :]


def scanned(core, place, own, other, ready, power, cov, length, parts):
    both, small, drift = ready
    n = cov.shape[0]
    square = jax.ShapeDtypeStruct((n, n), f32)
    vmem = pl.BlockSpec(memory_space=pltpu.VMEM)
    smem = pl.BlockSpec(memory_space=pltpu.SMEM)
    return pl.pallas_call(
        scan_kernel,
        out_shape=(
            jax.ShapeDtypeStruct((length, n), f32),
            jax.ShapeDtypeStruct((length // parts, n), f32),
            square, square, square,
        ),
        in_specs=[smem] * 2 + [vmem] * 7,
        out_specs=[vmem] * 5,
        scratch_shapes=[
            pltpu.VMEM((STEPS, length // STEPS, n), f32),
            pltpu.VMEM((STEPS, n, n), f32),
        ],
        compiler_params=pltpu.CompilerParams(vmem_limit_bytes=44 * 1024 * 1024),
        cost_estimate=pl.CostEstimate(flops=10**10, bytes_accessed=5 * 10**6, transcendentals=0),
        name="scan",
    )(core, place, own, other, both, small, power, cov, drift)


def swept(mats, n):
    row8 = lax.broadcasted_iota(jnp.int32, (8, n), 0)
    lane = lax.broadcasted_iota(jnp.int32, (1, n), 1)
    mats = [[m[8 * g : 8 * g + 8] for g in range(n // 8)] for m in mats]
    for k in range(n):
        found = []
        for m in mats:
            g, o = divmod(k, 8)
            pivot_row = m[g][o : o + 1, :]
            d = 1.0 / pivot_row[:, k : k + 1]
            s = jnp.where(lane == k, d, pivot_row * d)
            new = []
            for i, t in enumerate(m):
                u = jnp.where(lane == k, 0.0, t) - t[:, k : k + 1] * s
                new.append(jnp.where(row8 == o, s, u) if i == g else u)
            found.append(new)
        mats = found
    return [jnp.concatenate(m, axis=0) for m in mats]


def three(v, w):
    a, b, _ = thirds(v)
    c, d, _ = thirds(w)
    n = w.shape[1]
    y = plain(a, jnp.concatenate([c, d], axis=1))
    return y[:, :n] + (y[:, n:] + plain(b, c))


def inverse_kernel(total_ref, previous_ref, lagged_ref, cross_ref, loadings_ref, transition_ref):
    n = total_ref.shape[0]
    eye = (
        lax.broadcasted_iota(jnp.int32, (n, n), 0) == lax.broadcasted_iota(jnp.int32, (n, n), 1)
    ).astype(f32)
    mats = [total_ref[...], previous_ref[...]]
    near, left = [], []
    for m in mats:
        bound = jnp.max(jnp.sum(jnp.abs(m), axis=0, keepdims=True), axis=1, keepdims=True)
        r = eye - m * (1.8 / bound)
        left.append(r)
        near.append((eye + r) * (1.8 / bound))
    for _ in range(SQUARINGS):
        for i in range(2):
            left[i] = three(left[i], left[i])
            near[i] = near[i] + three(near[i], left[i])
    size = jnp.zeros((1, 1), f32)
    for i, (taken_ref, out_ref) in enumerate(
        ((cross_ref, loadings_ref), (lagged_ref, transition_ref))
    ):
        w = right(near[i])
        r = eye - times(mats[i], w)
        first = times(taken_ref[...], w)
        out_ref[...] = first + three(first, r)
        square = jnp.sum(jnp.sum(r * r, axis=0, keepdims=True), axis=1, keepdims=True)
        size = jnp.maximum(size, square)

    @pl.when(jnp.logical_not(size[0, 0] < 1e-6))
    def _():
        one, two = swept([total_ref[...], previous_ref[...]], n)
        loadings_ref[...] = high(cross_ref[...], one)
        transition_ref[...] = high(lagged_ref[...], two)


def inverted(total, previous, lagged, cross):
    vmem = pl.BlockSpec(memory_space=pltpu.VMEM)
    square = jax.ShapeDtypeStruct(total.shape, f32)
    return pl.pallas_call(
        inverse_kernel,
        out_shape=(jax.ShapeDtypeStruct(cross.shape, f32), square),
        in_specs=[vmem] * 4,
        out_specs=[vmem] * 2,
        compiler_params=pltpu.CompilerParams(vmem_limit_bytes=16 * 1024 * 1024),
        cost_estimate=pl.CostEstimate(flops=10**9, bytes_accessed=6 * 10**5, transcendentals=0),
        name="inverse",
    )(total, previous, lagged, cross)


def turned(value, axis, steps):
    count = lax.axis_size(axis)
    return lax.ppermute(value, axis, [(i, (i + steps) % count) for i in range(count)])


def over_z(value):
    count = lax.axis_size(Z)
    value = value + lax.ppermute(value, Z, [(i, i ^ 1) for i in range(count)])
    arrived = [turned(value, Z, 2 * k) for k in range(1, count // 2)]
    return sum(arrived, value)


def local(
    observations, loadings, noise_precision, transition, filter_cov, smoother_gain, smoothed_cov
):
    core = lax.axis_index(CORE)
    position = lax.axis_index(TM)
    length = observations.shape[0]
    width = transition.shape[0]
    half = length // 2
    groups = lax.axis_size((Y, X))
    rows = half // groups
    extra = width // groups
    kept_rows, given_rows, loadings, noise_precision = lax.optimization_barrier(
        (
            lax.dynamic_slice_in_dim(observations, core * half, half, 0),
            lax.dynamic_slice_in_dim(observations, (1 - core) * half, half, 0),
            loadings,
            noise_precision,
        )
    )
    weighted = noise_precision[:, None] * loadings
    factors = lax.optimization_barrier(weighted.astype(bf16))
    given = jnp.dot(given_rows, factors, preferred_element_type=f32)
    info_part = jnp.dot(loadings.T, weighted, precision=precise, preferred_element_type=f32)
    info_part = info_part + turned(info_part, CORE, 1)
    mine = jnp.dot(kept_rows, factors, preferred_element_type=f32)
    mine, info_part = lax.optimization_barrier((mine, info_part))
    mine = mine + turned(given, CORE, 1)
    pieces = jnp.concatenate(
        [mine.reshape(groups, rows, width), info_part.reshape(groups, extra, width)], axis=1
    )
    arrived = lax.all_to_all(pieces, (Y, X), split_axis=0, concat_axis=0, tiled=True)
    block = over_z(arrived.sum(axis=0))
    ready = readied(transition.T, filter_cov.T, smoother_gain.T, smoothed_cov, length)
    block, ready = lax.optimization_barrier((block, ready))
    copies = jnp.broadcast_to(block, (groups, *block.shape))
    own = lax.all_to_all(copies, (Y, X), split_axis=0, concat_axis=0, tiled=True)
    other = turned(own, CORE, 1)
    power = begun(own, filter_cov.T, transition.T)
    smoothed, shown, total, previous, lagged = scanned(
        core[None].astype(jnp.int32), position[None].astype(jnp.int32), own, other, ready,
        power, smoothed_cov, length, lax.axis_size(TM),
    )
    cross = jnp.einsum(
        "ts,tk->sk", observations, smoothed.astype(bf16), preferred_element_type=f32
    )
    new_loadings, new_transition = inverted(total, previous, lagged, cross)
    return (shown, new_loadings, new_transition)


def solution(mesh):
    split = Mesh(mesh.devices.reshape(4, 4, 2, mesh.shape["sr"]), (Y, X, CORE, Z))
    in_specs = (P(None, SR_TM), P(SR_TM, None), P(SR_TM), P(), P(), P(), P())
    out_specs = (P(TM, None), P(SR_TM, None), P())
    return jax.shard_map(local, mesh=split, in_specs=in_specs, out_specs=out_specs, check_vma=False)
```

```python
import jax
import jax.numpy as jnp
from jax import lax
from jax.experimental import pallas as pl
from jax.experimental.pallas import tpu as pltpu
from jax.sharding import Mesh
from jax.sharding import PartitionSpec as P

Y, X, CORE, Z = "tm_0", "tm_1", "tm_2", "sr"
TM = (Y, X, CORE)
SR_TM = (Z, Y, X, CORE)

STEPS = 8
SQUARINGS = 7
LEAPS = 8
FIRST = 4
f32 = jnp.float32
bf16 = jnp.bfloat16
precise = lax.Precision.HIGHEST


def thirds(v):
    a = v.astype(bf16)
    rest = v - a.astype(f32)
    b = rest.astype(bf16)
    c = (rest - b.astype(f32)).astype(bf16)
    return a, b, c


def right(w):
    a, b, c = thirds(w)
    both = jnp.concatenate([a, b], axis=1)
    if w.shape[0] <= 128:
        return both, (jnp.concatenate([c, a], axis=0),)
    return both, (c, a)


def plain(a, b):
    return jnp.dot(a, b, preferred_element_type=f32)


def times(v, w):
    return times_split(thirds(v), w)


def times_split(v, w):
    both, small = w
    n = both.shape[1] // 2
    a, b, c = v
    p, q = plain(a, both), plain(b, both)
    if len(small) == 1:
        least = plain(jnp.concatenate([a, c], axis=1), small[0])
    else:
        least = plain(a, small[0]) + plain(c, small[1])
    return p[:, :n] + (p[:, n:] + q[:, :n] + (q[:, n:] + least))


def high(a, b):
    return times(a, right(b))


def contracted(a, b):
    return lax.dot_general(a, b, (((0,), (0,)), ((), ())), preferred_element_type=f32)


def moved(v, shift, row):
    n = v.shape[0]
    keep = (row >= shift) if shift > 0 else (row < n + shift)
    return jnp.where(keep, pltpu.roll(v, shift % n, 0), 0.0)


def powers(a, n):
    found = [a]
    while len(found) < STEPS:
        more = high(jnp.concatenate(found, axis=0), found[-1])
        found = found + [more[i * n : (i + 1) * n] for i in range(len(found))]
    return found


def kept(blocks_at, count=1):
    both = blocks_at[0]
    small = blocks_at[1]
    if count == 1:
        return both, (jnp.concatenate([small, both[:, : both.shape[1] // 2]], axis=0),)
    return both, (small, both[:, : both.shape[1] // 2])


def beneath(*pieces):
    return tuple(jnp.concatenate(p, axis=0) for p in zip(*pieces))


def pieces_of(w):
    a, b, c = thirds(w)
    return jnp.concatenate([a, b], axis=1), c


def ready_kernel(ft_ref, kt_ref, jt_ref, cov_ref, both_ref, small_ref, drift_ref):
    n = ft_ref.shape[0]
    ft, kt, jt = ft_ref[...], kt_ref[...], jt_ref[...]
    eye = (
        lax.broadcasted_iota(jnp.int32, (n, n), 0) == lax.broadcasted_iota(jnp.int32, (n, n), 1)
    ).astype(f32)

    def put(at, w):
        both, small = pieces_of(w)
        both_ref[at] = both
        small_ref[at] = small

    put(0, kt)
    put(1, eye - high(ft, jt))
    raised = powers(jt, n)
    put(2, ft)
    put(3, high(ft, raised[-1]))
    for k, w in enumerate(raised):
        put(FIRST + k, w)
    power = raised[-1]
    for k in range(FIRST + STEPS, both_ref.shape[0]):
        power = high(power, power)
        put(k, power)
    drift_ref[...] = high(cov_ref[...], jt)


def readied(ft, kt, jt, cov, length):
    n = ft.shape[0]
    count = FIRST + STEPS + (length // STEPS).bit_length() - 2
    vmem = pl.BlockSpec(memory_space=pltpu.VMEM)
    return pl.pallas_call(
        ready_kernel,
        out_shape=(
            jax.ShapeDtypeStruct((count, n, 2 * n), bf16),
            jax.ShapeDtypeStruct((count, n, n), bf16),
            jax.ShapeDtypeStruct((n, n), f32),
        ),
        in_specs=[vmem] * 4,
        out_specs=[vmem] * 3,
        compiler_params=pltpu.CompilerParams(vmem_limit_bytes=16 * 1024 * 1024),
        cost_estimate=pl.CostEstimate(flops=10**9, bytes_accessed=2 * 10**6, transcendentals=0),
        name="ready",
    )(ft, kt, jt, cov)


def begin_kernel(own_ref, kt_ref, ft_ref, power_ref):
    n = ft_ref.shape[0]
    groups = own_ref.shape[0]
    rows = own_ref.shape[1] - n // groups
    info = jnp.concatenate([own_ref[g, rows:] for g in range(groups)], axis=0)
    ft = ft_ref[...]
    a = ft - high(high(ft, info), kt_ref[...])
    found = powers(a, n)
    for _ in range(LEAPS - 1):
        found.append(high(found[-1], found[-1]))
    for k, w in enumerate(found):
        power_ref[k] = w


def begun(own, kt, ft):
    n = ft.shape[0]
    vmem = pl.BlockSpec(memory_space=pltpu.VMEM)
    return pl.pallas_call(
        begin_kernel,
        out_shape=jax.ShapeDtypeStruct((STEPS + LEAPS - 1, n, n), f32),
        in_specs=[vmem] * 3,
        out_specs=vmem,
        compiler_params=pltpu.CompilerParams(vmem_limit_bytes=16 * 1024 * 1024),
        cost_estimate=pl.CostEstimate(flops=10**9, bytes_accessed=2 * 10**6, transcendentals=0),
        name="begin",
    )(own, kt, ft)


def scan_kernel(
    core_ref, place_ref, own_ref, other_ref, both_ref, small_ref, power_ref, cov_ref, drift_ref,
    x_ref, shown_ref, total_ref, previous_ref, lagged_ref, loc_ref, mat_ref,
):
    n = cov_ref.shape[0]
    groups = own_ref.shape[0]
    length = x_ref.shape[0]
    rows = length // (2 * groups)
    blocks = length // STEPS
    first = core_ref[0] == 0
    cov = cov_ref[...]
    held = lambda k: (both_ref[k], small_ref[k])
    pairs = blocks // 2
    row = lax.broadcasted_iota(jnp.int32, (pairs, n), 0)
    levels = blocks.bit_length() - 1
    leap = power_ref[STEPS + LEAPS - 2]
    leaps = [None] * (LEAPS - 1) + [right(leap)]

    def drive(j):
        def half(ref, start):
            parts = [
                ref[g, pl.ds(start, rows // (2 * STEPS), stride=2 * STEPS), :] for g in range(groups)
            ]
            return jnp.concatenate(parts, axis=0)

        found = []
        for start in (j, STEPS + j):
            own, other = half(own_ref, start), half(other_ref, start)
            found += [jnp.where(first, own, other), jnp.where(first, other, own)]
        return jnp.concatenate(found, axis=0)

    step = kept(beneath(pieces_of(power_ref[0]), held(0)), 2)
    state = times(drive(0), kept(held(0)))
    loc_ref[0] = state
    for j in range(1, STEPS):
        state = times(jnp.concatenate([state, drive(j)], axis=1), step)
        loc_ref[j] = state
        if len(leaps) < levels:
            leap = times(leap, leaps[-1])
            leaps.append(right(leap))
    even, odd = state[:pairs], state[pairs:]
    back = kept(beneath(held(FIRST), held(1)), 2)
    both = lambda j: jnp.concatenate([loc_ref[j], power_ref[j]], axis=0)

    def leap_of(level):
        nonlocal leap
        if level < LEAPS - 1:
            return right(power_ref[STEPS - 1 + level])
        if len(leaps) <= level:
            leap = times(leap, leaps[-1])
            leaps.append(right(leap))
        return leaps[level]

    enter = None
    level = 0
    out = times(both(STEPS - 1), kept(held(1)))
    for j in range(STEPS - 1, -1, -1):
        if j < STEPS - 1:
            out = times(jnp.concatenate([out, both(j)], axis=1), back)
        loc_ref[j] = out[:blocks]
        mat_ref[j] = out[blocks:]
        while level < (levels if j == 0 else STEPS - j):
            if level == 0:
                enter = times(even, leap_of(0)) + odd
            else:
                enter = enter + times(moved(enter, 1 << (level - 1), row), leap_of(level))
            level += 1
    entered = moved(enter, 1, row)
    e = jnp.concatenate([entered, times(entered, leap_of(0)) + even], axis=0)
    tail = lax.broadcasted_iota(jnp.int32, (8, n), 0) == 7
    final = jnp.where(tail, enter[pairs - 8 :], 0.0)
    after = times(final, kept(held(2)))
    z = loc_ref[0] + high(e, mat_ref[0])
    even = z[:pairs]
    odd = jnp.concatenate(
        [z[pairs : blocks - 8], z[blocks - 8 :] + times(final, kept(held(3)))], axis=0
    )
    one = kept(held(FIRST + STEPS - 1))
    even = even + times(odd, one)
    for level in range(levels - 1):
        even = even + times(moved(even, -(1 << level), row), kept(held(FIRST + STEPS + level)))
    ahead = moved(even, -1, row)
    odd = odd + times(ahead, one)
    z = jnp.concatenate([even, odd], axis=0)
    coming = jnp.concatenate([odd, ahead[: pairs - 8], ahead[pairs - 8 :] + after], axis=0)
    mixed = thirds(jnp.concatenate([e, coming], axis=1))
    sums = jnp.zeros((n, 2 * n), f32)

    def outer(x, prior):
        xa, xb = x
        pa, pb = prior
        pair = jnp.concatenate([xa, pa], axis=1)
        rest = jnp.concatenate([xb, pb], axis=1)
        return contracted(xa, pair) + (contracted(xb, pair) + contracted(xa, rest))

    opening = prior = thirds(z)[:2]

    def show(j, x):
        x_ref[pl.ds(j, pairs, stride=2 * STEPS), :] = x[:pairs]
        x_ref[pl.ds(STEPS + j, pairs, stride=2 * STEPS), :] = x[pairs:]

    show(0, z)
    for j in range(1, STEPS):
        w = kept(beneath(pieces_of(mat_ref[j]), held(FIRST + STEPS - 1 - j)), 2)
        x = loc_ref[j] + times_split(mixed, w)
        show(j, x)
        here = thirds(x)[:2]
        sums = sums + outer(here, prior)
        prior = here
    prior = jnp.concatenate([moved(x[pairs:], 1, row), x[:pairs]], axis=0)
    sums = sums + outer(opening, thirds(prior)[:2])
    last = jnp.where(tail, x_ref[length - 8 :], 0.0)
    la, lb, _ = thirds(last)
    ends = contracted(la, la) + (contracted(lb, la) + contracted(la, lb))
    total_ref[...] = sums[:, :n] + length * cov
    previous_ref[...] = (sums[:, :n] - ends) + (length - 1) * cov
    lagged_ref[...] = sums[:, n:] + (length - 1) * drift_ref[...]
    count = shown_ref.shape[0]
    shown_ref[...] = x_ref[pl.ds(pl.multiple_of(place_ref[0] * count, count), count), :]


def scanned(core, place, own, other, ready, power, cov, length, parts):
    both, small, drift = ready
    n = cov.shape[0]
    square = jax.ShapeDtypeStruct((n, n), f32)
    vmem = pl.BlockSpec(memory_space=pltpu.VMEM)
    smem = pl.BlockSpec(memory_space=pltpu.SMEM)
    return pl.pallas_call(
        scan_kernel,
        out_shape=(
            jax.ShapeDtypeStruct((length, n), f32),
            jax.ShapeDtypeStruct((length // parts, n), f32),
            square, square, square,
        ),
        in_specs=[smem] * 2 + [vmem] * 7,
        out_specs=[vmem] * 5,
        scratch_shapes=[
            pltpu.VMEM((STEPS, length // STEPS, n), f32),
            pltpu.VMEM((STEPS, n, n), f32),
        ],
        compiler_params=pltpu.CompilerParams(vmem_limit_bytes=44 * 1024 * 1024),
        cost_estimate=pl.CostEstimate(flops=10**10, bytes_accessed=5 * 10**6, transcendentals=0),
        name="scan",
    )(core, place, own, other, both, small, power, cov, drift)


def swept(mats, n):
    row8 = lax.broadcasted_iota(jnp.int32, (8, n), 0)
    lane = lax.broadcasted_iota(jnp.int32, (1, n), 1)
    mats = [[m[8 * g : 8 * g + 8] for g in range(n // 8)] for m in mats]
    for k in range(n):
        found = []
        for m in mats:
            g, o = divmod(k, 8)
            pivot_row = m[g][o : o + 1, :]
            d = 1.0 / pivot_row[:, k : k + 1]
            s = jnp.where(lane == k, d, pivot_row * d)
            new = []
            for i, t in enumerate(m):
                u = jnp.where(lane == k, 0.0, t) - t[:, k : k + 1] * s
                new.append(jnp.where(row8 == o, s, u) if i == g else u)
            found.append(new)
        mats = found
    return [jnp.concatenate(m, axis=0) for m in mats]


def three(v, w):
    a, b, _ = thirds(v)
    c, d, _ = thirds(w)
    n = w.shape[1]
    y = plain(a, jnp.concatenate([c, d], axis=1))
    return y[:, :n] + (y[:, n:] + plain(b, c))


def inverse_kernel(total_ref, previous_ref, lagged_ref, cross_ref, loadings_ref, transition_ref):
    n = total_ref.shape[0]
    eye = (
        lax.broadcasted_iota(jnp.int32, (n, n), 0) == lax.broadcasted_iota(jnp.int32, (n, n), 1)
    ).astype(f32)
    mats = [total_ref[...], previous_ref[...]]
    near, left = [], []
    for m in mats:
        bound = jnp.max(jnp.sum(jnp.abs(m), axis=0, keepdims=True), axis=1, keepdims=True)
        r = eye - m * (1.8 / bound)
        left.append(r)
        near.append((eye + r) * (1.8 / bound))
    for _ in range(SQUARINGS):
        for i in range(2):
            left[i] = three(left[i], left[i])
            near[i] = near[i] + three(near[i], left[i])
    size = jnp.zeros((1, 1), f32)
    for i, (taken_ref, out_ref) in enumerate(
        ((cross_ref, loadings_ref), (lagged_ref, transition_ref))
    ):
        w = right(near[i])
        r = eye - times(mats[i], w)
        first = times(taken_ref[...], w)
        out_ref[...] = first + three(first, r)
        square = jnp.sum(jnp.sum(r * r, axis=0, keepdims=True), axis=1, keepdims=True)
        size = jnp.maximum(size, square)

    @pl.when(jnp.logical_not(size[0, 0] < 1e-6))
    def _():
        one, two = swept([total_ref[...], previous_ref[...]], n)
        loadings_ref[...] = high(cross_ref[...], one)
        transition_ref[...] = high(lagged_ref[...], two)


def inverted(total, previous, lagged, cross):
    vmem = pl.BlockSpec(memory_space=pltpu.VMEM)
    square = jax.ShapeDtypeStruct(total.shape, f32)
    return pl.pallas_call(
        inverse_kernel,
        out_shape=(jax.ShapeDtypeStruct(cross.shape, f32), square),
        in_specs=[vmem] * 4,
        out_specs=[vmem] * 2,
        compiler_params=pltpu.CompilerParams(vmem_limit_bytes=16 * 1024 * 1024),
        cost_estimate=pl.CostEstimate(flops=10**9, bytes_accessed=6 * 10**5, transcendentals=0),
        name="inverse",
    )(total, previous, lagged, cross)


def turned(value, axis, steps):
    count = lax.axis_size(axis)
    return lax.ppermute(value, axis, [(i, (i + steps) % count) for i in range(count)])


def over_z(value):
    count = lax.axis_size(Z)
    value = value + lax.ppermute(value, Z, [(i, i ^ 1) for i in range(count)])
    arrived = [turned(value, Z, 2 * k) for k in range(1, count // 2)]
    return sum(arrived, value)


def local(
    observations, loadings, noise_precision, transition, filter_cov, smoother_gain, smoothed_cov
):
    core = lax.axis_index(CORE)
    position = lax.axis_index(TM)
    length = observations.shape[0]
    width = transition.shape[0]
    half = length // 2
    groups = lax.axis_size((Y, X))
    rows = half // groups
    extra = width // groups
    kept_rows, given_rows, loadings, noise_precision = lax.optimization_barrier(
        (
            lax.dynamic_slice_in_dim(observations, core * half, half, 0),
            lax.dynamic_slice_in_dim(observations, (1 - core) * half, half, 0),
            loadings,
            noise_precision,
        )
    )
    weighted = noise_precision[:, None] * loadings
    factors = lax.optimization_barrier(weighted.astype(bf16))
    given = jnp.dot(given_rows, factors, preferred_element_type=f32)
    info_part = jnp.dot(loadings.T, weighted, precision=precise, preferred_element_type=f32)
    info_part = info_part + turned(info_part, CORE, 1)
    mine = jnp.dot(kept_rows, factors, preferred_element_type=f32)
    mine, info_part = lax.optimization_barrier((mine, info_part))
    mine = mine + turned(given, CORE, 1)
    pieces = jnp.concatenate(
        [mine.reshape(groups, rows, width), info_part.reshape(groups, extra, width)], axis=1
    )
    arrived = lax.all_to_all(pieces, (Y, X), split_axis=0, concat_axis=0, tiled=True)
    block = over_z(arrived.sum(axis=0))
    ready = readied(transition.T, filter_cov.T, smoother_gain.T, smoothed_cov, length)
    block, ready = lax.optimization_barrier((block, ready))
    copies = jnp.broadcast_to(block, (groups, *block.shape))
    own = lax.all_to_all(copies, (Y, X), split_axis=0, concat_axis=0, tiled=True)
    other = turned(own, CORE, 1)
    power = begun(own, filter_cov.T, transition.T)
    smoothed, shown, total, previous, lagged = scanned(
        core[None].astype(jnp.int32), position[None].astype(jnp.int32), own, other, ready,
        power, smoothed_cov, length, lax.axis_size(TM),
    )
    cross = jnp.einsum(
        "ts,tk->sk", observations, smoothed.astype(bf16), preferred_element_type=f32
    )
    new_loadings, new_transition = inverted(total, previous, lagged, cross)
    return (shown, new_loadings, new_transition)


def solution(mesh):
    split = Mesh(mesh.devices.reshape(4, 4, 2, mesh.shape["sr"]), (Y, X, CORE, Z))
    in_specs = (P(None, SR_TM), P(SR_TM, None), P(SR_TM), P(), P(), P(), P())
    out_specs = (P(TM, None), P(SR_TM, None), P())
    return jax.shard_map(local, mesh=split, in_specs=in_specs, out_specs=out_specs, check_vma=False)
```
